256 devices in a mesh: space: 32 (over x, z), rep: 8 (over y, core).
Axes of the slice: x: 4, y: 4, z: 8, core: 2. Of those that a mesh axis runs over, the one named last changes fastest.
Arguments:
- feats: bfloat16 [8, 128, 64, 512], P('rep', 'space'), may hold values from -6 to 6
- cotangent: bfloat16 [8, 128, 64, 512], P('rep', 'space'), may hold values from -6 to 6
- weight: bfloat16 [27, 64, 64], replicated, may hold values from -0.15625 to 0.15625
- bias: float32 [64], replicated, may hold values from -3 to 3
- neighbours: int32 [8, 128, 26], P('rep', 'space'), may hold values from -1 to 127, as said below
- occupancy: int32 [8, 128, 512], P('rep', 'space'), may hold values from 0 to 1, as said below
Outputs:
- out_feats: bfloat16 [8, 128, 64, 512], P('rep', 'space')
- in_grad: bfloat16 [8, 128, 64, 512], P('rep', 'space')
- weight_grad: float32 [27, 64, 64], replicated
- bias_grad: float32 [64], replicated
The draws below stay inside these ranges and needn't reach their ends.
Inputs may be any that keep to these rules, and one draw needn't show every extreme that they name: Slot s of a district lies on space index s // 4. On each space index the live bricks fill the first slots; a live brick has at least one occupied voxel and a dead slot none. A brick of a district lies in the slab of its space index at one of 8 x 8 positions; neighbours[s, j] is the slot of the live brick adjacent in direction j, which lies on space index s // 4 + dx; dead slots list only -1, and the lists are symmetric. In every district some space index holds 4 live bricks. `occupancy`: dead slots are all zero.
All inputs are finite; a program needn't handle non-finite values.
Results may differ from the reference program's by a relative error of at most 0.0085.
Values may be sent and summed in bfloat16 or wider, within the bound.
A program may use at most 128 MiB of HBM per device.

```python
import math
import jax
import jax.numpy as jnp
from jax import lax

C = 64
B_DEV = 4
GRID = 8
BRICKS = 128
DISTRICTS = 8


DIRECTIONS = [(a, b, c) for a in (-1, 0, 1) for b in (-1, 0, 1) for c in (-1, 0, 1) if (a, b, c) != (0, 0, 0)]


def layout(key):
    base = jax.random.fold_in(key, 11)
    subkeys = jax.random.split(base, 4)
    devices = BRICKS // B_DEV
    places = GRID * GRID
    live_count = jax.random.randint(subkeys[0], (DISTRICTS, devices), 1, B_DEV + 1)
    fullest = jax.random.randint(subkeys[1], (DISTRICTS, 1), 0, devices)
    live_count = jnp.where(jnp.arange(devices)[None, :] == fullest, B_DEV, live_count).astype(jnp.int32)
    scores = jax.random.randint(subkeys[2], (DISTRICTS, devices, places), 0, 1 << 20) * places + jnp.arange(places)[None, None, :]
    slot_places = jnp.argsort(scores, axis=-1).astype(jnp.int32)
    place_slots = jnp.argsort(slot_places, axis=-1).astype(jnp.int32)
    return (live_count, slot_places, place_slots, subkeys[3])


def draw_neighbours(key, part):
    live_count, slot_places, place_slots, leftover = layout(key)
    devices = BRICKS // B_DEV
    places = GRID * GRID
    shape3 = (DISTRICTS, devices, B_DEV)
    position = slot_places[:, :, :B_DEV]
    row_index = position // GRID
    col_index = position % GRID
    own_live = jnp.arange(B_DEV)[None, None, :] < live_count[:, :, None]
    device = jnp.broadcast_to(jnp.arange(devices)[None, :, None], shape3)
    flat_slots = place_slots.reshape(DISTRICTS, devices * places)
    columns = []
    for a, b, c in DIRECTIONS:
        there_dev = device + a
        new_row = row_index + b
        new_col = col_index + c
        inside = (there_dev >= 0) & (there_dev < devices) & (new_row >= 0) & (new_row < GRID) & (new_col >= 0) & (new_col < GRID)
        there_clip = jnp.clip(there_dev, 0, devices - 1)
        place_clip = jnp.clip(new_row, 0, GRID - 1) * GRID + jnp.clip(new_col, 0, GRID - 1)
        flat_index = (there_clip * places + place_clip).reshape(DISTRICTS, -1)
        target_slot = jnp.take_along_axis(flat_slots, flat_index, axis=1).reshape(shape3)
        live_there = jnp.take_along_axis(live_count, there_clip.reshape(DISTRICTS, -1), axis=1).reshape(shape3)
        usable = inside & own_live & (target_slot < live_there)
        columns.append(jnp.where(usable, there_clip * B_DEV + target_slot, -1))
    return jnp.stack(columns, axis=-1).reshape(DISTRICTS, BRICKS, 26).astype(jnp.int32)


def draw_occupancy(key, part):
    live_count, slot_places, place_slots, leftover = layout(key)
    subkeys = jax.random.split(leftover, 3)
    percent = jax.random.randint(subkeys[0], (DISTRICTS, BRICKS, 1), 20, 91)
    rolled = jax.random.randint(subkeys[1], (DISTRICTS, BRICKS, 512), 0, 100)
    forced = jax.random.randint(subkeys[2], (DISTRICTS, BRICKS, 1), 0, 512)
    own_live = (jnp.arange(B_DEV)[None, None, :] < live_count[:, :, None]).reshape(DISTRICTS, BRICKS, 1)
    filled = ((rolled < percent) | (jnp.arange(512)[None, None, :] == forced)) & own_live
    return filled.astype(jnp.int32)


def steps_of(stream_key, dims, shards, least, top_value):
    factor_of, own = 1.0, jax.random.fold_in(stream_key, 6)
    for axis_at, blocks in shards:
        draws = jnp.exp(jax.random.uniform(jax.random.fold_in(own, axis_at), (blocks,), jnp.float32, least / len(shards), top_value / len(shards)))
        factor_of = factor_of * jnp.repeat(draws, dims[axis_at] // blocks).reshape([-1 if axis == axis_at else 1 for axis in range(len(dims))])
    return factor_of


def noise(stream_key, shape, deviation, reach, pieces=(), held_as=jnp.bfloat16):
    entries = jax.random.normal(stream_key, shape, jnp.float32) * deviation
    if len(pieces) > 0:
        entries = steps_of(stream_key, shape, pieces, -0.22, 0.18) * entries
    return jnp.clip(entries, min=-reach, max=reach).astype(held_as)


def setup_inputs(seed: int = 0) -> dict:
    seeds = jax.random.split(jax.random.key(seed), 7)
    return {
        "feats": noise(seeds[0], (DISTRICTS, BRICKS, C, 512), 1.0, 6.0, ((0, 8), (1, 32))),
        "cotangent": noise(seeds[1], (DISTRICTS, BRICKS, C, 512), 1.0, 6.0, ((0, 8), (1, 32))),
        "weight": noise(seeds[2], (27, C, C), (27 * C) ** -0.5, 0.15625),
        "bias": noise(seeds[3], (C,), 0.5, 3.0, (), jnp.float32),
        "neighbours": draw_neighbours(jax.random.fold_in(seeds[6], 71), 0),
        "occupancy": draw_occupancy(jax.random.fold_in(seeds[6], 71), 0),
    }


DIRECTIONS = [(a, b, c) for a in (-1, 0, 1) for b in (-1, 0, 1) for c in (-1, 0, 1) if (a, b, c) != (0, 0, 0)]

def extent(shift_step):
    if shift_step < 0:
        return (slice(7, 8), slice(0, 1))
    if shift_step == 0:
        return (slice(0, 8), slice(1, 9))
    return (slice(0, 1), slice(9, 10))

def surround(bricks_cube, targets):
    slot_count = bricks_cube.shape[0]
    padded = jnp.zeros(bricks_cube.shape[:2] + (10, 10, 10), bricks_cube.dtype)
    padded = padded.at[:, :, 1:9, 1:9, 1:9].set(bricks_cube)
    for direction, (a, b, c) in enumerate(DIRECTIONS):
        take_x, put_x = extent(a)
        take_y, put_y = extent(b)
        take_z, put_z = extent(c)
        chosen = targets[:, direction]
        source = jnp.take(bricks_cube[:, :, take_x, take_y, take_z], jnp.clip(chosen, 0, slot_count - 1).astype(jnp.int32), axis=0)
        source = jnp.where((chosen >= 0)[:, None, None, None, None], source, jnp.zeros((), bricks_cube.dtype))
        padded = padded.at[:, :, put_x, put_y, put_z].set(source)
    return padded

def convolve(padded, weight, bias):
    slot_count, channels = (padded.shape[0], padded.shape[1])
    summed = jnp.zeros((slot_count, channels, 512), jnp.float32) + bias[None, :, None]
    for a in range(3):
        for b in range(3):
            for c in range(3):
                shifted = padded[:, :, a:a + 8, b:b + 8, c:c + 8].reshape(slot_count, channels, 512).astype(jnp.float32)
                summed = summed + jnp.einsum('oi,niv->nov', weight[9 * a + 3 * b + c].astype(jnp.float32), shifted)
    return summed

def back_convolve(padded_grad, weight):
    slot_count, channels = (padded_grad.shape[0], padded_grad.shape[1])
    summed = jnp.zeros((slot_count, channels, 512), jnp.float32)
    for a in range(3):
        for b in range(3):
            for c in range(3):
                shifted = padded_grad[:, :, 2 - a:10 - a, 2 - b:10 - b, 2 - c:10 - c].reshape(slot_count, channels, 512).astype(jnp.float32)
                summed = summed + jnp.einsum('oi,nov->niv', weight[9 * a + 3 * b + c].astype(jnp.float32), shifted)
    return summed

def weight_products(grad_pre, padded):
    slot_count, channels = (padded.shape[0], padded.shape[1])
    grad_float = grad_pre.astype(jnp.float32)
    terms_list = []
    for a in range(3):
        for b in range(3):
            for c in range(3):
                shifted = padded[:, :, a:a + 8, b:b + 8, c:c + 8].reshape(slot_count, channels, 512).astype(jnp.float32)
                terms_list.append(jnp.einsum('nov,niv->oi', grad_float, shifted))
    return jnp.stack(terms_list)

def reference(feats, cotangent, weight, bias, neighbours, occupancy):

    def district(inputs):
        features, incoming, targets, filled = inputs
        slot_count, channels = (features.shape[0], features.shape[1])
        masked = features * filled.astype(jnp.bfloat16)[:, None, :]
        keep_float = filled.astype(jnp.float32)[:, None, :]
        padded = surround(masked.reshape(slot_count, channels, 8, 8, 8), targets)
        preact = convolve(padded, weight, bias)
        sigmoid_pre = jax.nn.sigmoid(preact)
        result = (masked.astype(jnp.float32) + keep_float * preact * sigmoid_pre).astype(jnp.bfloat16)
        grad_pre = (incoming.astype(jnp.float32) * keep_float * sigmoid_pre * (1.0 + preact * (1.0 - sigmoid_pre))).astype(jnp.bfloat16)
        padded_grad = surround(grad_pre.reshape(slot_count, channels, 8, 8, 8), targets)
        returned = back_convolve(padded_grad, weight)
        in_grad = (keep_float * (incoming.astype(jnp.float32) + returned)).astype(jnp.bfloat16)
        weight_terms = weight_products(grad_pre, padded)
        bias_terms = lax.optimization_barrier(jnp.sum(grad_pre.astype(jnp.float32), axis=(0, 2)))
        return (result, in_grad, weight_terms, bias_terms)
    result, in_grad, weight_terms, bias_terms = lax.map(district, (feats, cotangent, neighbours, occupancy))
    normaliser = 1.0 / math.sqrt(DISTRICTS * BRICKS * 512)
    return (result, in_grad, lax.optimization_barrier(jnp.sum(weight_terms, axis=0)) * normaliser, lax.optimization_barrier(jnp.sum(bias_terms, axis=0)) * normaliser)
```

```python
import math

import jax
import jax.numpy as jnp
from jax import lax
from jax.sharding import PartitionSpec as P

DIRECTIONS = [
    (a, b, c) for a in (-1, 0, 1) for b in (-1, 0, 1) for c in (-1, 0, 1) if (a, b, c) != (0, 0, 0)
]


def padded_2(array, sides, width):
    for axis, dim in sides:
        size, length = (lax.axis_size(axis), array.shape[dim])
        up = [(i, (i + 1) % size) for i in range(size - 1)]
        down = [(j, i) for i, j in up]
        last = lax.slice_in_dim(array, length - width, length, axis=dim)
        initial = lax.slice_in_dim(array, 0, width, axis=dim)
        before = lax.ppermute(last, axis, up)
        after = lax.ppermute(initial, axis, down)
        array = jnp.concatenate([before, array, after], axis=dim)
    return array


def extent(shift_step):
    if shift_step < 0:
        return (slice(7, 8), slice(0, 1))
    if shift_step == 0:
        return (slice(0, 8), slice(1, 9))
    return (slice(0, 1), slice(9, 10))


def boundary(bricks):
    slot_count, channels = (bricks.shape[0], bricks.shape[1])
    layered = bricks.reshape(slot_count, channels, 8, 64)
    low_plane = layered[:, :, 0, :].reshape(slot_count, channels * 64)
    high_plane = layered[:, :, 7, :].reshape(slot_count, channels * 64)
    return jnp.stack([low_plane, high_plane])


def surround(bricks, face_rows, targets, my_index):
    slot_count, channels = (bricks.shape[0], bricks.shape[1])
    bricks_cube = bricks.reshape(slot_count, channels, 8, 8, 8)
    lower_faces = face_rows[0].reshape(slot_count, channels, 1, 8, 8)
    upper_faces = face_rows[3].reshape(slot_count, channels, 1, 8, 8)
    padded = jnp.zeros((slot_count, channels, 10, 10, 10), bricks.dtype)
    padded = padded.at[:, :, 1:9, 1:9, 1:9].set(bricks_cube)
    for direction, (a, b, c) in enumerate(DIRECTIONS):
        take_x, put_x = extent(a)
        take_y, put_y = extent(b)
        take_z, put_z = extent(c)
        if a == 0:
            lookup = bricks_cube[:, :, take_x, take_y, take_z]
        elif a < 0:
            lookup = lower_faces[:, :, :, take_y, take_z]
        else:
            lookup = upper_faces[:, :, :, take_y, take_z]
        chosen = targets[:, direction]
        local_slot = jnp.clip(chosen - (my_index + a) * slot_count, 0, slot_count - 1)
        source = jnp.take(lookup, local_slot, axis=0)
        source = jnp.where(
            (chosen >= 0)[:, None, None, None, None], source, jnp.zeros((), bricks.dtype)
        )
        padded = padded.at[:, :, put_x, put_y, put_z].set(source)
    return padded


def depth_planes(padded):
    slot_count, channels = (padded.shape[0], padded.shape[1])
    return [padded[:, :, :, :, c : c + 8].reshape(slot_count, channels, 10, 80) for c in range(3)]


def shifted_field(planes, a, b, c):
    piece = planes[c][:, :, a : a + 8, 8 * b : 8 * b + 64]
    return piece.reshape(piece.shape[0], piece.shape[1], 512)


def convolve(planes, weight, bias):
    slot_count, channels = (planes[0].shape[0], planes[0].shape[1])
    summed = jnp.zeros((slot_count, channels, 512), jnp.float32) + bias[None, :, None]
    for a in range(3):
        for b in range(3):
            for c in range(3):
                summed = summed + jnp.einsum(
                    "oi,niv->nov",
                    weight[9 * a + 3 * b + c],
                    shifted_field(planes, a, b, c),
                    preferred_element_type=jnp.float32,
                )
    return summed


def back_convolve(grad_planes, weight):
    slot_count, channels = (grad_planes[0].shape[0], grad_planes[0].shape[1])
    summed = jnp.zeros((slot_count, channels, 512), jnp.float32)
    for a in range(3):
        for b in range(3):
            for c in range(3):
                summed = summed + jnp.einsum(
                    "oi,nov->niv",
                    weight[9 * a + 3 * b + c],
                    shifted_field(grad_planes, 2 - a, 2 - b, 2 - c),
                    preferred_element_type=jnp.float32,
                )
    return summed


def weight_products(grad_pre, planes):
    terms_list = []
    for a in range(3):
        for b in range(3):
            for c in range(3):
                terms_list.append(
                    jnp.einsum(
                        "nov,niv->oi",
                        grad_pre,
                        shifted_field(planes, a, b, c),
                        preferred_element_type=jnp.float32,
                    )
                )
    return jnp.stack(terms_list)


SUM_AXES = ("space", "rep")


def all_sum(weight_terms, bias_terms):
    flat = jnp.concatenate([weight_terms.reshape(-1), bias_terms])
    count = lax.axis_size(SUM_AXES)
    rep_size = lax.axis_size("rep")
    me = lax.axis_index("space") * rep_size + lax.axis_index("rep")
    bits = [b for b in (0, 1, 3, 6, 2, 4, 7, 5) if (1 << b) < count]
    whole = flat.shape[0]
    padded = -(-whole // count) * count
    x = jnp.pad(flat, (0, padded - whole))
    for b in bits:
        bit = (me >> b) & 1
        halves = x.reshape(2, -1)
        keep = jnp.where(bit == 0, halves[0], halves[1])
        send = jnp.where(bit == 0, halves[1], halves[0])
        pairs = [(i, i ^ (1 << b)) for i in range(count)]
        x = keep + lax.ppermute(send, SUM_AXES, pairs)
    for b in reversed(bits):
        bit = (me >> b) & 1
        pairs = [(i, i ^ (1 << b)) for i in range(count)]
        other = lax.ppermute(x, SUM_AXES, pairs)
        x = jnp.where(bit == 0, jnp.concatenate([x, other]), jnp.concatenate([other, x]))
    x = x[:whole]
    return x[: weight_terms.size].reshape(weight_terms.shape), x[weight_terms.size :]


def on_device(feats, cotangent, weight, bias, neighbours, occupancy):
    filled = occupancy[0]
    neighbour_ids = neighbours[0]
    incoming = cotangent[0]
    slot_count, channels = (feats.shape[1], feats.shape[2])
    my_index = lax.axis_index("space")
    masked = feats[0] * filled.astype(jnp.bfloat16)[:, None, :]
    keep_float = filled.astype(jnp.float32)[:, None, :]
    face_rows = padded_2(boundary(masked), (("space", 0),), 1)
    planes = depth_planes(surround(masked, face_rows, neighbour_ids, my_index))
    preact = convolve(planes, weight, bias)
    sigmoid_pre = jax.nn.sigmoid(preact)
    result = (masked.astype(jnp.float32) + keep_float * preact * sigmoid_pre).astype(jnp.bfloat16)
    grad_pre = (
        incoming.astype(jnp.float32)
        * keep_float
        * sigmoid_pre
        * (1.0 + preact * (1.0 - sigmoid_pre))
    ).astype(jnp.bfloat16)
    grad_rows = padded_2(boundary(grad_pre), (("space", 0),), 1)
    grad_planes = depth_planes(surround(grad_pre, grad_rows, neighbour_ids, my_index))
    returned = back_convolve(grad_planes, weight)
    weight_terms = weight_products(grad_pre, planes)
    in_grad = (keep_float * (incoming.astype(jnp.float32) + returned)).astype(jnp.bfloat16)
    bias_terms = jnp.sum(grad_pre.astype(jnp.float32), axis=(0, 2))
    weight_total, bias_total = all_sum(weight_terms, bias_terms)
    normaliser = 1.0 / math.sqrt(
        feats.shape[0] * lax.axis_size("rep") * slot_count * lax.axis_size("space") * 512
    )
    return (result[None], in_grad[None], weight_total * normaliser, bias_total * normaliser)


def solution(mesh):
    placed = (
        P("rep", "space", None, None),
        P("rep", "space", None, None),
        P(),
        P(),
        P("rep", "space", None),
        P("rep", "space", None),
    )
    return jax.shard_map(
        on_device,
        mesh=mesh,
        in_specs=placed,
        out_specs=(P("rep", "space", None, None), P("rep", "space", None, None), P(), P()),
        check_vma=False,
    )
```

```python
import functools
import math

import jax
import jax.numpy as jnp
from jax import lax
from jax.experimental import pallas as pl
from jax.experimental.pallas import tpu as pltpu
from jax.sharding import PartitionSpec as P

INTERPRET = False

DIRECTIONS = [
    (a, b, c) for a in (-1, 0, 1) for b in (-1, 0, 1) for c in (-1, 0, 1) if (a, b, c) != (0, 0, 0)
]
OFFSETS = [(a - 1, b - 1, c - 1) for a in range(3) for b in range(3) for c in range(3)]
STRIDES = (64, 8, 1)
ZERO_SLOT = 12


def offset_terms(shift):
    moving = [axis for axis in range(3) if shift[axis] != 0]
    terms = []
    for pick in range(1 << len(moving)):
        out_axes = [axis for n, axis in enumerate(moving) if (pick >> n) & 1]
        direction = tuple(shift[axis] if axis in out_axes else 0 for axis in range(3))
        flat = sum(STRIDES[axis] * (shift[axis] - (8 * shift[axis] if axis in out_axes else 0)) for axis in range(3))
        pattern = [(axis, shift[axis], axis in out_axes) for axis in moving]
        terms.append((direction, (-flat) % 512, pattern))
    return terms


def gather_columns(src_ref, tbl_ref, brick, col_ref, sign, edges):
    base = brick * 26
    for k, off in enumerate(OFFSETS):
        shift = tuple(sign * s for s in off)
        val = None
        for direction, roll, pattern in offset_terms(shift):
            if direction == (0, 0, 0):
                field = src_ref[brick].astype(jnp.float32)
            else:
                slot = tbl_ref[base + DIRECTIONS.index(direction)]
                field = src_ref[slot].astype(jnp.float32)
            if roll:
                field = pltpu.roll(field, roll, 1)
            if val is None:
                val = field
                continue
            mask = None
            for axis, step, out in pattern:
                m = edges[(axis, step)] if out else jnp.logical_not(edges[(axis, step)])
                mask = m if mask is None else jnp.logical_and(mask, m)
            val = jnp.where(mask, field, val)
        col_ref[pl.ds(k * 64, 64), :] = val.astype(jnp.bfloat16)


def edge_masks(shape):
    v = lax.broadcasted_iota(jnp.int32, shape, 1)
    coords = (v >> 6, (v >> 3) & 7, v & 7)
    edges = {}
    for axis in range(3):
        edges[(axis, -1)] = coords[axis] == 0
        edges[(axis, 1)] = coords[axis] == 7
    return edges


def forward_kernel(tbl_ref, x_ref, cot_ref, occ_ref, w_ref, bias_ref, out_ref, gp_ref, dw_ref, db_ref, col_ref):
    slots, channels, voxels = cot_ref.shape
    edges = edge_masks((channels, voxels))
    dw_ref[...] = jnp.zeros_like(dw_ref)
    db_ref[...] = jnp.zeros_like(db_ref)

    def brick_step(brick, carry):
        gather_columns(x_ref, tbl_ref, brick, col_ref, 1, edges)
        pre = jnp.dot(w_ref[...], col_ref[...], preferred_element_type=jnp.float32) + bias_ref[...]
        sig = 1.0 / (1.0 + jnp.exp(-pre))
        keep = occ_ref[brick]
        masked = x_ref[brick].astype(jnp.float32)
        out_ref[brick] = (masked + keep * pre * sig).astype(out_ref.dtype)
        gp = (cot_ref[brick].astype(jnp.float32) * keep * sig * (1.0 + pre * (1.0 - sig))).astype(jnp.bfloat16)
        gp_ref[brick] = gp
        dw_ref[...] += lax.dot_general(
            gp, col_ref[...], (((1,), (1,)), ((), ())), preferred_element_type=jnp.float32
        )
        db_ref[...] += jnp.sum(gp.astype(jnp.float32), axis=1, keepdims=True)
        return carry

    lax.fori_loop(0, slots, brick_step, 0)


def backward_kernel(tbl_ref, g_ref, cot_ref, occ_ref, wt_ref, in_grad_ref, col_ref):
    slots, channels, voxels = cot_ref.shape
    edges = edge_masks((channels, voxels))

    def brick_step(brick, carry):
        gather_columns(g_ref, tbl_ref, brick, col_ref, -1, edges)
        back = jnp.dot(wt_ref[...], col_ref[...], preferred_element_type=jnp.float32)
        keep = occ_ref[brick]
        in_grad_ref[brick] = (keep * (cot_ref[brick].astype(jnp.float32) + back)).astype(in_grad_ref.dtype)
        return carry

    lax.fori_loop(0, slots, brick_step, 0)


def vmem_specs(n):
    return [pl.BlockSpec(memory_space=pltpu.VMEM)] * n


def run_forward(tbl, table, cot, occ, w_all, bias):
    slots, channels, voxels = cot.shape
    return pl.pallas_call(
        forward_kernel,
        out_shape=(
            jax.ShapeDtypeStruct((slots, channels, voxels), jnp.bfloat16),
            jax.ShapeDtypeStruct((slots, channels, voxels), jnp.bfloat16),
            jax.ShapeDtypeStruct((channels, 27 * channels), jnp.float32),
            jax.ShapeDtypeStruct((channels, 1), jnp.float32),
        ),
        in_specs=[pl.BlockSpec(memory_space=pltpu.SMEM)] + vmem_specs(5),
        out_specs=tuple(vmem_specs(4)),
        scratch_shapes=[pltpu.VMEM((27 * channels, voxels), jnp.bfloat16)],
        interpret=INTERPRET,
    )(tbl, table, cot, occ, w_all, bias)


def run_backward(tbl, table, cot, occ, w_t):
    slots, channels, voxels = cot.shape
    return pl.pallas_call(
        backward_kernel,
        out_shape=jax.ShapeDtypeStruct((slots, channels, voxels), jnp.bfloat16),
        in_specs=[pl.BlockSpec(memory_space=pltpu.SMEM)] + vmem_specs(4),
        out_specs=pl.BlockSpec(memory_space=pltpu.VMEM),
        scratch_shapes=[pltpu.VMEM((27 * channels, voxels), jnp.bfloat16)],
        interpret=INTERPRET,
    )(tbl, table, cot, occ, w_t)


def exchange_planes(field):
    size = lax.axis_size("space")
    up = [(i, i + 1) for i in range(size - 1)]
    down = [(i + 1, i) for i in range(size - 1)]
    voxels = field.shape[-1]
    low = field[:, :, :64]
    high = field[:, :, voxels - 64 :]
    from_left = lax.ppermute(high, "space", up)
    from_right = lax.ppermute(low, "space", down)
    left = jnp.pad(from_left, ((0, 0), (0, 0), (voxels - 64, 0)))
    right = jnp.pad(from_right, ((0, 0), (0, 0), (0, voxels - 64)))
    zero = jnp.zeros((1,) + field.shape[1:], field.dtype)
    return jnp.concatenate([field, left, right, zero])


def slot_table(neighbour_ids, my_index):
    slots = neighbour_ids.shape[0]
    dx = jnp.array([d[0] for d in DIRECTIONS], jnp.int32)[None, :]
    local = neighbour_ids - (my_index + dx) * slots
    base = jnp.where(dx == 0, 0, jnp.where(dx < 0, slots, 2 * slots))
    table = jnp.where(neighbour_ids >= 0, base + jnp.clip(local, 0, slots - 1), 3 * slots)
    return table.reshape(-1).astype(jnp.int32)


SUM_AXES = ("space", "rep")


def all_sum(weight_terms, bias_terms):
    flat = jnp.concatenate([weight_terms.reshape(-1), bias_terms])
    count = lax.axis_size(SUM_AXES)
    rep_size = lax.axis_size("rep")
    me = lax.axis_index("space") * rep_size + lax.axis_index("rep")
    bits = [b for b in (0, 1, 3, 6, 2, 4, 7, 5) if (1 << b) < count]
    whole = flat.shape[0]
    padded = -(-whole // count) * count
    x = jnp.pad(flat, (0, padded - whole))
    for b in bits:
        bit = (me >> b) & 1
        halves = x.reshape(2, -1)
        keep = jnp.where(bit == 0, halves[0], halves[1])
        send = jnp.where(bit == 0, halves[1], halves[0])
        pairs = [(i, i ^ (1 << b)) for i in range(count)]
        x = keep + lax.ppermute(send, SUM_AXES, pairs)
    for b in reversed(bits):
        bit = (me >> b) & 1
        pairs = [(i, i ^ (1 << b)) for i in range(count)]
        other = lax.ppermute(x, SUM_AXES, pairs)
        x = jnp.where(bit == 0, jnp.concatenate([x, other]), jnp.concatenate([other, x]))
    x = x[:whole]
    return x[: weight_terms.size].reshape(weight_terms.shape), x[weight_terms.size :]


def on_device(feats, cotangent, weight, bias, neighbours, occupancy):
    filled = occupancy[0]
    incoming = cotangent[0]
    slot_count, channels = (feats.shape[1], feats.shape[2])
    my_index = lax.axis_index("space")
    masked = feats[0] * filled.astype(jnp.bfloat16)[:, None, :]
    keep_float = filled.astype(jnp.float32)[:, None, :]
    tbl = slot_table(neighbours[0], my_index)
    w_all = weight.transpose(1, 0, 2).reshape(channels, 27 * channels)
    w_t = weight.transpose(2, 0, 1).reshape(channels, 27 * channels)
    result, grad_pre, dw, db = run_forward(
        tbl, exchange_planes(masked), incoming, keep_float, w_all, bias.reshape(channels, 1)
    )
    in_grad = run_backward(tbl, exchange_planes(grad_pre), incoming, keep_float, w_t)
    weight_terms = dw.reshape(channels, 27, channels).transpose(1, 0, 2)
    weight_total, bias_total = all_sum(weight_terms, db.reshape(channels))
    normaliser = 1.0 / math.sqrt(
        feats.shape[0] * lax.axis_size("rep") * slot_count * lax.axis_size("space") * 512
    )
    return (result[None], in_grad[None], weight_total * normaliser, bias_total * normaliser)


def solution(mesh):
    placed = (
        P("rep", "space", None, None),
        P("rep", "space", None, None),
        P(),
        P(),
        P("rep", "space", None),
        P("rep", "space", None),
    )
    return jax.shard_map(
        on_device,
        mesh=mesh,
        in_specs=placed,
        out_specs=(P("rep", "space", None, None), P("rep", "space", None, None), P(), P()),
        check_vma=False,
    )
```

```python
import functools
import math

import jax
import jax.numpy as jnp
from jax import lax
from jax.experimental import pallas as pl
from jax.experimental.pallas import tpu as pltpu
from jax.sharding import PartitionSpec as P

INTERPRET = False
REMOTE_INTERPRET = False

DIRECTIONS = [
    (a, b, c) for a in (-1, 0, 1) for b in (-1, 0, 1) for c in (-1, 0, 1) if (a, b, c) != (0, 0, 0)
]
OFFSETS = [(a - 1, b - 1, c - 1) for a in range(3) for b in range(3) for c in range(3)]
STRIDES = (64, 8, 1)
ZERO_SLOT = 12


def offset_terms(shift):
    moving = [axis for axis in range(3) if shift[axis] != 0]
    terms = []
    for pick in range(1 << len(moving)):
        out_axes = [axis for n, axis in enumerate(moving) if (pick >> n) & 1]
        direction = tuple(shift[axis] if axis in out_axes else 0 for axis in range(3))
        flat = sum(STRIDES[axis] * (shift[axis] - (8 * shift[axis] if axis in out_axes else 0)) for axis in range(3))
        pattern = [(axis, shift[axis], axis in out_axes) for axis in moving]
        terms.append((direction, (-flat) % 512, pattern))
    return terms


def gather_columns(src_ref, tbl_ref, brick, col_ref, sign, edges):
    base = brick * 26
    for k, off in enumerate(OFFSETS):
        shift = tuple(sign * s for s in off)
        val = None
        for direction, roll, pattern in offset_terms(shift):
            if direction == (0, 0, 0):
                field = src_ref[brick].astype(jnp.float32)
            else:
                slot = tbl_ref[base + DIRECTIONS.index(direction)]
                field = src_ref[slot].astype(jnp.float32)
            if roll:
                field = pltpu.roll(field, roll, 1)
            if val is None:
                val = field
                continue
            mask = None
            for axis, step, out in pattern:
                m = edges[(axis, step)] if out else jnp.logical_not(edges[(axis, step)])
                mask = m if mask is None else jnp.logical_and(mask, m)
            val = jnp.where(mask, field, val)
        col_ref[pl.ds(k * 64, 64), :] = val.astype(jnp.bfloat16)


def edge_masks(shape):
    v = lax.broadcasted_iota(jnp.int32, shape, 1)
    coords = (v >> 6, (v >> 3) & 7, v & 7)
    edges = {}
    for axis in range(3):
        edges[(axis, -1)] = coords[axis] == 0
        edges[(axis, 1)] = coords[axis] == 7
    return edges


def forward_kernel(tbl_ref, x_ref, cot_ref, occ_ref, w_ref, bias_ref, out_ref, gp_ref, dw_ref, db_ref, col_ref):
    slots, channels, voxels = cot_ref.shape
    edges = edge_masks((channels, voxels))
    dw_ref[...] = jnp.zeros_like(dw_ref)
    db_ref[...] = jnp.zeros_like(db_ref)

    def brick_step(brick, carry):
        gather_columns(x_ref, tbl_ref, brick, col_ref, 1, edges)
        pre = jnp.dot(w_ref[...], col_ref[...], preferred_element_type=jnp.float32) + bias_ref[...]
        sig = 1.0 / (1.0 + jnp.exp(-pre))
        keep = occ_ref[brick]
        masked = x_ref[brick].astype(jnp.float32)
        out_ref[brick] = (masked + keep * pre * sig).astype(out_ref.dtype)
        gp = (cot_ref[brick].astype(jnp.float32) * keep * sig * (1.0 + pre * (1.0 - sig))).astype(jnp.bfloat16)
        gp_ref[brick] = gp
        dw_ref[...] += lax.dot_general(
            gp, col_ref[...], (((1,), (1,)), ((), ())), preferred_element_type=jnp.float32
        )
        db_ref[...] += jnp.sum(gp.astype(jnp.float32), axis=1, keepdims=True)
        return carry

    lax.fori_loop(0, slots, brick_step, 0)


def backward_kernel(tbl_ref, g_ref, cot_ref, occ_ref, wt_ref, in_grad_ref, col_ref):
    slots, channels, voxels = cot_ref.shape
    edges = edge_masks((channels, voxels))

    def brick_step(brick, carry):
        gather_columns(g_ref, tbl_ref, brick, col_ref, -1, edges)
        back = jnp.dot(wt_ref[...], col_ref[...], preferred_element_type=jnp.float32)
        keep = occ_ref[brick]
        in_grad_ref[brick] = (keep * (cot_ref[brick].astype(jnp.float32) + back)).astype(in_grad_ref.dtype)
        return carry

    lax.fori_loop(0, slots, brick_step, 0)


def vmem_specs(n):
    return [pl.BlockSpec(memory_space=pltpu.VMEM)] * n


def run_forward(tbl, table, cot, occ, w_all, bias):
    slots, channels, voxels = cot.shape
    return pl.pallas_call(
        forward_kernel,
        out_shape=(
            jax.ShapeDtypeStruct((slots, channels, voxels), jnp.bfloat16),
            jax.ShapeDtypeStruct((slots, channels, voxels), jnp.bfloat16),
            jax.ShapeDtypeStruct((channels, 27 * channels), jnp.float32),
            jax.ShapeDtypeStruct((channels, 1), jnp.float32),
        ),
        in_specs=[pl.BlockSpec(memory_space=pltpu.SMEM)] + vmem_specs(5),
        out_specs=tuple(vmem_specs(4)),
        scratch_shapes=[pltpu.VMEM((27 * channels, voxels), jnp.bfloat16)],
        interpret=INTERPRET,
    )(tbl, table, cot, occ, w_all, bias)


def run_backward(tbl, table, cot, occ, w_t):
    slots, channels, voxels = cot.shape
    return pl.pallas_call(
        backward_kernel,
        out_shape=jax.ShapeDtypeStruct((slots, channels, voxels), jnp.bfloat16),
        in_specs=[pl.BlockSpec(memory_space=pltpu.SMEM)] + vmem_specs(4),
        out_specs=pl.BlockSpec(memory_space=pltpu.VMEM),
        scratch_shapes=[pltpu.VMEM((27 * channels, voxels), jnp.bfloat16)],
        interpret=INTERPRET,
    )(tbl, table, cot, occ, w_t)


def exchange_planes(field):
    size = lax.axis_size("space")
    up = [(i, i + 1) for i in range(size - 1)]
    down = [(i + 1, i) for i in range(size - 1)]
    voxels = field.shape[-1]
    low = field[:, :, :64]
    high = field[:, :, voxels - 64 :]
    from_left = lax.ppermute(high, "space", up)
    from_right = lax.ppermute(low, "space", down)
    left = jnp.pad(from_left, ((0, 0), (0, 0), (voxels - 64, 0)))
    right = jnp.pad(from_right, ((0, 0), (0, 0), (0, voxels - 64)))
    zero = jnp.zeros((1,) + field.shape[1:], field.dtype)
    return jnp.concatenate([field, left, right, zero])


def slot_table(neighbour_ids, my_index):
    slots = neighbour_ids.shape[0]
    dx = jnp.array([d[0] for d in DIRECTIONS], jnp.int32)[None, :]
    local = neighbour_ids - (my_index + dx) * slots
    base = jnp.where(dx == 0, 0, jnp.where(dx < 0, slots, 2 * slots))
    table = jnp.where(neighbour_ids >= 0, base + jnp.clip(local, 0, slots - 1), 3 * slots)
    return table.reshape(-1).astype(jnp.int32)


SUM_AXES = ("space", "rep")
SUM_ORDER = (0, 1, 3, 6, 2, 4, 7, 5)


def partner_of(me, bit, rep_size):
    own = (me // (1 << bit)) % 2
    other = me + (1 - 2 * own) * (1 << bit)
    return own, (other // rep_size, other % rep_size)


def reduce_kernel(bits, rep_size, x_ref, o_ref, buf, recv, full, send_sem, recv_sem, local_sem):
    rows = buf.shape[0]
    me = lax.axis_index("space") * rep_size + lax.axis_index("rep")
    mesh_ids = pl.DeviceIdType.MESH
    barrier = pltpu.get_barrier_semaphore()
    for bit in bits:
        pl.semaphore_signal(barrier, 1, device_id=partner_of(me, bit, rep_size)[1], device_id_type=mesh_ids)
    pl.semaphore_wait(barrier, len(bits))
    first = pltpu.make_async_copy(x_ref, buf, local_sem)
    first.start()
    first.wait()
    lo = 0
    length = rows
    for step, bit in enumerate(bits[:-1]):
        own, device = partner_of(me, bit, rep_size)
        half = length // 2
        keep_lo = pl.multiple_of(lo + own * half, 8)
        send_lo = pl.multiple_of(lo + (1 - own) * half, 8)
        at = rows - (rows >> step)
        copy = pltpu.make_async_remote_copy(
            src_ref=buf.at[pl.ds(send_lo, half)],
            dst_ref=recv.at[pl.ds(at, half)],
            send_sem=send_sem.at[step],
            recv_sem=recv_sem.at[step],
            device_id=device,
            device_id_type=mesh_ids,
        )
        copy.start()
        copy.wait()
        buf[pl.ds(keep_lo, half)] += recv[pl.ds(at, half)]
        lo = keep_lo
        length = half
    last = len(bits) - 1
    own, device = partner_of(me, bits[last], rep_size)
    at = rows - length
    copy = pltpu.make_async_remote_copy(
        src_ref=buf.at[pl.ds(lo, length)],
        dst_ref=recv.at[pl.ds(at, length)],
        send_sem=send_sem.at[last],
        recv_sem=recv_sem.at[last],
        device_id=device,
        device_id_type=mesh_ids,
    )
    copy.start()
    copy.wait()
    full[pl.ds(lo, length)] = buf[pl.ds(lo, length)] + recv[pl.ds(at, length)]
    for step in reversed(range(last)):
        own, device = partner_of(me, bits[step], rep_size)
        copy = pltpu.make_async_remote_copy(
            src_ref=full.at[pl.ds(lo, length)],
            dst_ref=full.at[pl.ds(lo, length)],
            send_sem=send_sem.at[last + 1 + step],
            recv_sem=recv_sem.at[last + 1 + step],
            device_id=device,
            device_id_type=mesh_ids,
        )
        copy.start()
        copy.wait()
        lo = pl.multiple_of(lo - own * length, 8)
        length = 2 * length
    o_ref[...] = full[...]


def all_sum(weight_terms, bias_terms):
    flat = jnp.concatenate([weight_terms.reshape(-1), bias_terms])
    count = lax.axis_size(SUM_AXES)
    rep_size = lax.axis_size("rep")
    bits = tuple(b for b in SUM_ORDER if (1 << b) < count)
    unit = 8 << (len(bits) - 1)
    whole = flat.shape[0]
    rows = -(-(-(-whole // 128)) // unit) * unit
    x = jnp.pad(flat, (0, rows * 128 - whole)).reshape(rows, 128)
    steps = 2 * len(bits) - 1
    summed = pl.pallas_call(
        functools.partial(reduce_kernel, bits, rep_size),
        out_shape=jax.ShapeDtypeStruct((rows, 128), jnp.float32),
        in_specs=[pl.BlockSpec(memory_space=pltpu.VMEM)],
        out_specs=pl.BlockSpec(memory_space=pltpu.VMEM),
        scratch_shapes=[
            pltpu.VMEM((rows, 128), jnp.float32),
            pltpu.VMEM((rows, 128), jnp.float32),
            pltpu.VMEM((rows, 128), jnp.float32),
            pltpu.SemaphoreType.DMA((steps,)),
            pltpu.SemaphoreType.DMA((steps,)),
            pltpu.SemaphoreType.DMA(()),
        ],
        compiler_params=pltpu.CompilerParams(collective_id=0, has_side_effects=True),
        interpret=REMOTE_INTERPRET,
    )(x)
    x = summed.reshape(-1)[:whole]
    return x[: weight_terms.size].reshape(weight_terms.shape), x[weight_terms.size :]


def on_device(feats, cotangent, weight, bias, neighbours, occupancy):
    filled = occupancy[0]
    incoming = cotangent[0]
    slot_count, channels = (feats.shape[1], feats.shape[2])
    my_index = lax.axis_index("space")
    masked = feats[0] * filled.astype(jnp.bfloat16)[:, None, :]
    keep_float = filled.astype(jnp.float32)[:, None, :]
    tbl = slot_table(neighbours[0], my_index)
    w_all = weight.transpose(1, 0, 2).reshape(channels, 27 * channels)
    w_t = weight.transpose(2, 0, 1).reshape(channels, 27 * channels)
    result, grad_pre, dw, db = run_forward(
        tbl, exchange_planes(masked), incoming, keep_float, w_all, bias.reshape(channels, 1)
    )
    in_grad = run_backward(tbl, exchange_planes(grad_pre), incoming, keep_float, w_t)
    weight_terms = dw.reshape(channels, 27, channels).transpose(1, 0, 2)
    weight_total, bias_total = all_sum(weight_terms, db.reshape(channels))
    normaliser = 1.0 / math.sqrt(
        feats.shape[0] * lax.axis_size("rep") * slot_count * lax.axis_size("space") * 512
    )
    return (result[None], in_grad[None], weight_total * normaliser, bias_total * normaliser)


def solution(mesh):
    placed = (
        P("rep", "space", None, None),
        P("rep", "space", None, None),
        P(),
        P(),
        P("rep", "space", None),
        P("rep", "space", None),
    )
    return jax.shard_map(
        on_device,
        mesh=mesh,
        in_specs=placed,
        out_specs=(P("rep", "space", None, None), P("rep", "space", None, None), P(), P()),
        check_vma=False,
    )
```

```python
import functools
import math

import jax
import jax.numpy as jnp
from jax import lax
from jax.experimental import pallas as pl
from jax.experimental.pallas import tpu as pltpu
from jax.sharding import PartitionSpec as P

INTERPRET = False
REMOTE_INTERPRET = False

DIRECTIONS = [
    (a, b, c) for a in (-1, 0, 1) for b in (-1, 0, 1) for c in (-1, 0, 1) if (a, b, c) != (0, 0, 0)
]
OFFSETS = [(a - 1, b - 1, c - 1) for a in range(3) for b in range(3) for c in range(3)]
STRIDES = (64, 8, 1)
ZERO_SLOT = 12


def offset_terms(shift):
    moving = [axis for axis in range(3) if shift[axis] != 0]
    terms = []
    for pick in range(1 << len(moving)):
        out_axes = [axis for n, axis in enumerate(moving) if (pick >> n) & 1]
        direction = tuple(shift[axis] if axis in out_axes else 0 for axis in range(3))
        flat = sum(STRIDES[axis] * (shift[axis] - (8 * shift[axis] if axis in out_axes else 0)) for axis in range(3))
        pattern = [(axis, shift[axis], axis in out_axes) for axis in moving]
        terms.append((direction, (-flat) % 512, pattern))
    return terms


def gather_columns(src_ref, tbl_ref, brick, col_ref, sign, edges):
    base = brick * 26
    for k, off in enumerate(OFFSETS):
        shift = tuple(sign * s for s in off)
        val = None
        for direction, roll, pattern in offset_terms(shift):
            if direction == (0, 0, 0):
                field = src_ref[brick].astype(jnp.float32)
            else:
                slot = tbl_ref[base + DIRECTIONS.index(direction)]
                field = src_ref[slot].astype(jnp.float32)
            if roll:
                field = pltpu.roll(field, roll, 1)
            if val is None:
                val = field
                continue
            mask = None
            for axis, step, out in pattern:
                m = edges[(axis, step)] if out else jnp.logical_not(edges[(axis, step)])
                mask = m if mask is None else jnp.logical_and(mask, m)
            val = jnp.where(mask, field, val)
        col_ref[pl.ds(k * 64, 64), :] = val.astype(jnp.bfloat16)


def edge_masks(shape):
    v = lax.broadcasted_iota(jnp.int32, shape, 1)
    coords = (v >> 6, (v >> 3) & 7, v & 7)
    edges = {}
    for axis in range(3):
        edges[(axis, -1)] = coords[axis] == 0
        edges[(axis, 1)] = coords[axis] == 7
    return edges


def forward_kernel(tbl_ref, x_ref, cot_ref, occ_ref, w_ref, bias_ref, out_ref, gp_ref, dw_ref, db_ref, col_ref):
    slots, channels, voxels = cot_ref.shape
    edges = edge_masks((channels, voxels))
    dw_ref[...] = jnp.zeros_like(dw_ref)
    db_ref[...] = jnp.zeros_like(db_ref)

    def brick_step(brick, carry):
        gather_columns(x_ref, tbl_ref, brick, col_ref, 1, edges)
        pre = jnp.dot(w_ref[...], col_ref[...], preferred_element_type=jnp.float32) + bias_ref[...]
        sig = 1.0 / (1.0 + jnp.exp(-pre))
        keep = occ_ref[brick]
        masked = x_ref[brick].astype(jnp.float32)
        out_ref[brick] = (masked + keep * pre * sig).astype(out_ref.dtype)
        gp = (cot_ref[brick].astype(jnp.float32) * keep * sig * (1.0 + pre * (1.0 - sig))).astype(jnp.bfloat16)
        gp_ref[brick] = gp
        dw_ref[...] += lax.dot_general(
            gp, col_ref[...], (((1,), (1,)), ((), ())), preferred_element_type=jnp.float32
        )
        db_ref[...] += jnp.sum(gp.astype(jnp.float32), axis=1, keepdims=True)
        return carry

    lax.fori_loop(0, slots, brick_step, 0)


def backward_brick(tbl_ref, g_ref, cot_ref, occ_ref, wt_ref, in_grad_ref, col_ref, edges, brick):
    gather_columns(g_ref, tbl_ref, brick, col_ref, -1, edges)
    back = jnp.dot(wt_ref[...], col_ref[...], preferred_element_type=jnp.float32)
    keep = occ_ref[brick]
    in_grad_ref[brick] = (keep * (cot_ref[brick].astype(jnp.float32) + back)).astype(in_grad_ref.dtype)


def vmem_specs(n):
    return [pl.BlockSpec(memory_space=pltpu.VMEM)] * n


def run_forward(tbl, table, cot, occ, w_all, bias):
    slots, channels, voxels = cot.shape
    return pl.pallas_call(
        forward_kernel,
        out_shape=(
            jax.ShapeDtypeStruct((slots, channels, voxels), jnp.bfloat16),
            jax.ShapeDtypeStruct((slots, channels, voxels), jnp.bfloat16),
            jax.ShapeDtypeStruct((channels, 27 * channels), jnp.float32),
            jax.ShapeDtypeStruct((channels, 1), jnp.float32),
        ),
        in_specs=[pl.BlockSpec(memory_space=pltpu.SMEM)] + vmem_specs(5),
        out_specs=tuple(vmem_specs(4)),
        scratch_shapes=[pltpu.VMEM((27 * channels, voxels), jnp.bfloat16)],
        interpret=INTERPRET,
    )(tbl, table, cot, occ, w_all, bias)


def exchange_planes(field):
    size = lax.axis_size("space")
    up = [(i, i + 1) for i in range(size - 1)]
    down = [(i + 1, i) for i in range(size - 1)]
    voxels = field.shape[-1]
    low = field[:, :, :64]
    high = field[:, :, voxels - 64 :]
    from_left = lax.ppermute(high, "space", up)
    from_right = lax.ppermute(low, "space", down)
    left = jnp.pad(from_left, ((0, 0), (0, 0), (voxels - 64, 0)))
    right = jnp.pad(from_right, ((0, 0), (0, 0), (0, voxels - 64)))
    zero = jnp.zeros((1,) + field.shape[1:], field.dtype)
    return jnp.concatenate([field, left, right, zero])


def slot_table(neighbour_ids, my_index):
    slots = neighbour_ids.shape[0]
    dx = jnp.array([d[0] for d in DIRECTIONS], jnp.int32)[None, :]
    local = neighbour_ids - (my_index + dx) * slots
    base = jnp.where(dx == 0, 0, jnp.where(dx < 0, slots, 2 * slots))
    table = jnp.where(neighbour_ids >= 0, base + jnp.clip(local, 0, slots - 1), 3 * slots)
    return table.reshape(-1).astype(jnp.int32)


SUM_AXES = ("space", "rep")
SUM_ORDER = (0, 1, 3, 6, 2, 4, 7, 5)


def partner_of(me, bit, rep_size):
    own = (me // (1 << bit)) % 2
    other = me + (1 - 2 * own) * (1 << bit)
    return own, (other // rep_size, other % rep_size)


def reduce_kernel(
    bits, rep_size, tbl_ref, x_ref, g_ref, cot_ref, occ_ref, wt_ref, o_ref, in_grad_ref,
    buf, recv, full, col_ref, send_sem, recv_sem, local_sem,
):
    rows = buf.shape[0]
    slots, channels, voxels = cot_ref.shape
    edges = edge_masks((channels, voxels))
    me = lax.axis_index("space") * rep_size + lax.axis_index("rep")
    mesh_ids = pl.DeviceIdType.MESH
    barrier = pltpu.get_barrier_semaphore()
    for bit in bits:
        pl.semaphore_signal(barrier, 1, device_id=partner_of(me, bit, rep_size)[1], device_id_type=mesh_ids)
    pl.semaphore_wait(barrier, len(bits))
    first = pltpu.make_async_copy(x_ref, buf, local_sem)
    first.start()
    first.wait()
    lo = 0
    length = rows
    for step, bit in enumerate(bits[:-1]):
        own, device = partner_of(me, bit, rep_size)
        half = length // 2
        keep_lo = pl.multiple_of(lo + own * half, 8)
        send_lo = pl.multiple_of(lo + (1 - own) * half, 8)
        at = rows - (rows >> step)
        copy = pltpu.make_async_remote_copy(
            src_ref=buf.at[pl.ds(send_lo, half)],
            dst_ref=recv.at[pl.ds(at, half)],
            send_sem=send_sem.at[step],
            recv_sem=recv_sem.at[step],
            device_id=device,
            device_id_type=mesh_ids,
        )
        copy.start()
        for brick in range(step, slots, len(bits) - 1) if step < slots else ():
            backward_brick(tbl_ref, g_ref, cot_ref, occ_ref, wt_ref, in_grad_ref, col_ref, edges, brick)
        copy.wait()
        buf[pl.ds(keep_lo, half)] += recv[pl.ds(at, half)]
        lo = keep_lo
        length = half
    last = len(bits) - 1
    own, device = partner_of(me, bits[last], rep_size)
    at = rows - length
    copy = pltpu.make_async_remote_copy(
        src_ref=buf.at[pl.ds(lo, length)],
        dst_ref=recv.at[pl.ds(at, length)],
        send_sem=send_sem.at[last],
        recv_sem=recv_sem.at[last],
        device_id=device,
        device_id_type=mesh_ids,
    )
    copy.start()
    copy.wait()
    full[pl.ds(lo, length)] = buf[pl.ds(lo, length)] + recv[pl.ds(at, length)]
    for step in reversed(range(last)):
        own, device = partner_of(me, bits[step], rep_size)
        copy = pltpu.make_async_remote_copy(
            src_ref=full.at[pl.ds(lo, length)],
            dst_ref=full.at[pl.ds(lo, length)],
            send_sem=send_sem.at[last + 1 + step],
            recv_sem=recv_sem.at[last + 1 + step],
            device_id=device,
            device_id_type=mesh_ids,
        )
        copy.start()
        copy.wait()
        lo = pl.multiple_of(lo - own * length, 8)
        length = 2 * length
    o_ref[...] = full[...]


def all_sum_and_backward(weight_terms, bias_terms, tbl, grad_table, incoming, keep_float, w_t):
    flat = jnp.concatenate([weight_terms.reshape(-1), bias_terms])
    count = lax.axis_size(SUM_AXES)
    rep_size = lax.axis_size("rep")
    bits = tuple(b for b in SUM_ORDER if (1 << b) < count)
    unit = 8 << (len(bits) - 1)
    whole = flat.shape[0]
    rows = -(-(-(-whole // 128)) // unit) * unit
    x = jnp.pad(flat, (0, rows * 128 - whole)).reshape(rows, 128)
    steps = 2 * len(bits) - 1
    slots, channels, voxels = incoming.shape
    summed, in_grad = pl.pallas_call(
        functools.partial(reduce_kernel, bits, rep_size),
        out_shape=(
            jax.ShapeDtypeStruct((rows, 128), jnp.float32),
            jax.ShapeDtypeStruct((slots, channels, voxels), jnp.bfloat16),
        ),
        in_specs=[pl.BlockSpec(memory_space=pltpu.SMEM)] + vmem_specs(5),
        out_specs=tuple(vmem_specs(2)),
        scratch_shapes=[
            pltpu.VMEM((rows, 128), jnp.float32),
            pltpu.VMEM((rows, 128), jnp.float32),
            pltpu.VMEM((rows, 128), jnp.float32),
            pltpu.VMEM((27 * channels, voxels), jnp.bfloat16),
            pltpu.SemaphoreType.DMA((steps,)),
            pltpu.SemaphoreType.DMA((steps,)),
            pltpu.SemaphoreType.DMA(()),
        ],
        compiler_params=pltpu.CompilerParams(collective_id=0, has_side_effects=True),
        interpret=REMOTE_INTERPRET,
    )(tbl, x, grad_table, incoming, keep_float, w_t)
    x = summed.reshape(-1)[:whole]
    return x[: weight_terms.size].reshape(weight_terms.shape), x[weight_terms.size :], in_grad


def on_device(feats, cotangent, weight, bias, neighbours, occupancy):
    filled = occupancy[0]
    incoming = cotangent[0]
    slot_count, channels = (feats.shape[1], feats.shape[2])
    my_index = lax.axis_index("space")
    masked = feats[0] * filled.astype(jnp.bfloat16)[:, None, :]
    keep_float = filled.astype(jnp.float32)[:, None, :]
    tbl = slot_table(neighbours[0], my_index)
    w_all = weight.transpose(1, 0, 2).reshape(channels, 27 * channels)
    w_t = weight.transpose(2, 0, 1).reshape(channels, 27 * channels)
    result, grad_pre, dw, db = run_forward(
        tbl, exchange_planes(masked), incoming, keep_float, w_all, bias.reshape(channels, 1)
    )
    weight_terms = dw.reshape(channels, 27, channels).transpose(1, 0, 2)
    weight_total, bias_total, in_grad = all_sum_and_backward(
        weight_terms, db.reshape(channels), tbl, exchange_planes(grad_pre), incoming, keep_float, w_t
    )
    normaliser = 1.0 / math.sqrt(
        feats.shape[0] * lax.axis_size("rep") * slot_count * lax.axis_size("space") * 512
    )
    return (result[None], in_grad[None], weight_total * normaliser, bias_total * normaliser)


def solution(mesh):
    placed = (
        P("rep", "space", None, None),
        P("rep", "space", None, None),
        P(),
        P(),
        P("rep", "space", None),
        P("rep", "space", None),
    )
    return jax.shard_map(
        on_device,
        mesh=mesh,
        in_specs=placed,
        out_specs=(P("rep", "space", None, None), P("rep", "space", None, None), P(), P()),
        check_vma=False,
    )
```

```python
import functools
import math

import jax
import jax.numpy as jnp
from jax import lax
from jax.experimental import pallas as pl
from jax.experimental.pallas import tpu as pltpu
from jax.sharding import PartitionSpec as P

INTERPRET = False
REMOTE_INTERPRET = False

DIRECTIONS = [
    (a, b, c) for a in (-1, 0, 1) for b in (-1, 0, 1) for c in (-1, 0, 1) if (a, b, c) != (0, 0, 0)
]
OFFSETS = [(a - 1, b - 1, c - 1) for a in range(3) for b in range(3) for c in range(3)]
STRIDES = (64, 8, 1)
ZERO_SLOT = 12


def offset_terms(shift):
    moving = [axis for axis in range(3) if shift[axis] != 0]
    terms = []
    for pick in range(1 << len(moving)):
        out_axes = [axis for n, axis in enumerate(moving) if (pick >> n) & 1]
        direction = tuple(shift[axis] if axis in out_axes else 0 for axis in range(3))
        flat = sum(STRIDES[axis] * (shift[axis] - (8 * shift[axis] if axis in out_axes else 0)) for axis in range(3))
        pattern = [(axis, shift[axis], axis in out_axes) for axis in moving]
        terms.append((direction, (-flat) % 512, pattern))
    return terms


def gather_columns(src_ref, tbl_ref, brick, col_ref, sign, edges):
    base = brick * 26
    for k, off in enumerate(OFFSETS):
        shift = tuple(sign * s for s in off)
        val = None
        for direction, roll, pattern in offset_terms(shift):
            if direction == (0, 0, 0):
                field = src_ref[brick]
            else:
                slot = tbl_ref[base + DIRECTIONS.index(direction)]
                field = src_ref[slot]
            if roll:
                field = pltpu.roll(field, roll, 1)
            if val is None:
                val = field
                continue
            mask = None
            for axis, step, out in pattern:
                m = edges[(axis, step)] if out else jnp.logical_not(edges[(axis, step)])
                mask = m if mask is None else jnp.logical_and(mask, m)
            val = jnp.where(mask, field, val)
        col_ref[pl.ds(k * 64, 64), :] = val


def edge_masks(shape):
    v = lax.broadcasted_iota(jnp.int32, shape, 1)
    coords = (v >> 6, (v >> 3) & 7, v & 7)
    edges = {}
    for axis in range(3):
        edges[(axis, -1)] = coords[axis] == 0
        edges[(axis, 1)] = coords[axis] == 7
    return edges


def forward_kernel(tbl_ref, x_ref, cot_ref, occ_ref, w_ref, bias_ref, out_ref, gp_ref, dw_ref, db_ref, col_ref):
    slots, channels, voxels = cot_ref.shape
    edges = edge_masks((1, voxels))
    dw_ref[...] = jnp.zeros_like(dw_ref)
    db_ref[...] = jnp.zeros_like(db_ref)

    def brick_step(brick, carry):
        gather_columns(x_ref, tbl_ref, brick, col_ref, 1, edges)
        pre = jnp.dot(w_ref[...], col_ref[...], preferred_element_type=jnp.float32) + bias_ref[...]
        sig = 1.0 / (1.0 + jnp.exp(-pre))
        keep = occ_ref[brick]
        masked = x_ref[brick].astype(jnp.float32)
        out_ref[brick] = (masked + keep * pre * sig).astype(out_ref.dtype)
        gp = (cot_ref[brick].astype(jnp.float32) * keep * sig * (1.0 + pre * (1.0 - sig))).astype(jnp.bfloat16)
        gp_ref[brick] = gp
        dw_ref[...] += lax.dot_general(
            gp, col_ref[...], (((1,), (1,)), ((), ())), preferred_element_type=jnp.float32
        )
        db_ref[...] += jnp.sum(gp.astype(jnp.float32), axis=1, keepdims=True)
        return carry

    lax.fori_loop(0, slots, brick_step, 0)


def backward_brick(tbl_ref, g_ref, cot_ref, occ_ref, wt_ref, in_grad_ref, col_ref, edges, brick):
    gather_columns(g_ref, tbl_ref, brick, col_ref, -1, edges)
    back = jnp.dot(wt_ref[...], col_ref[...], preferred_element_type=jnp.float32)
    keep = occ_ref[brick]
    in_grad_ref[brick] = (keep * (cot_ref[brick].astype(jnp.float32) + back)).astype(in_grad_ref.dtype)


def vmem_specs(n):
    return [pl.BlockSpec(memory_space=pltpu.VMEM)] * n


def run_forward(tbl, table, cot, occ, w_all, bias):
    slots, channels, voxels = cot.shape
    return pl.pallas_call(
        forward_kernel,
        out_shape=(
            jax.ShapeDtypeStruct((slots, channels, voxels), jnp.bfloat16),
            jax.ShapeDtypeStruct((slots, channels, voxels), jnp.bfloat16),
            jax.ShapeDtypeStruct((channels, 27 * channels), jnp.float32),
            jax.ShapeDtypeStruct((channels, 1), jnp.float32),
        ),
        in_specs=[pl.BlockSpec(memory_space=pltpu.SMEM)] + vmem_specs(5),
        out_specs=tuple(vmem_specs(4)),
        scratch_shapes=[pltpu.VMEM((27 * channels, voxels), jnp.bfloat16)],
        interpret=INTERPRET,
    )(tbl, table, cot, occ, w_all, bias)


def exchange_planes(field):
    size = lax.axis_size("space")
    up = [(i, i + 1) for i in range(size - 1)]
    down = [(i + 1, i) for i in range(size - 1)]
    voxels = field.shape[-1]
    low = field[:, :, :64]
    high = field[:, :, voxels - 64 :]
    from_left = lax.ppermute(high, "space", up)
    from_right = lax.ppermute(low, "space", down)
    left = jnp.pad(from_left, ((0, 0), (0, 0), (voxels - 64, 0)))
    right = jnp.pad(from_right, ((0, 0), (0, 0), (0, voxels - 64)))
    zero = jnp.zeros((1,) + field.shape[1:], field.dtype)
    return jnp.concatenate([field, left, right, zero])


def slot_table(neighbour_ids, my_index):
    slots = neighbour_ids.shape[0]
    dx = jnp.array([d[0] for d in DIRECTIONS], jnp.int32)[None, :]
    local = neighbour_ids - (my_index + dx) * slots
    base = jnp.where(dx == 0, 0, jnp.where(dx < 0, slots, 2 * slots))
    table = jnp.where(neighbour_ids >= 0, base + jnp.clip(local, 0, slots - 1), 3 * slots)
    return table.reshape(-1).astype(jnp.int32)


SUM_AXES = ("space", "rep")


def sum_levels(space_size, rep_size):
    z_size = 8 if space_size % 8 == 0 else space_size
    space_i = lax.axis_index("space")
    rep_i = lax.axis_index("rep")
    x_i, z_i = space_i // z_size, space_i % z_size
    levels = []
    if rep_size > 1:
        levels.append((rep_size, rep_i, lambda p: (space_i, p)))
    if z_size > 1:
        levels.append((z_size, z_i, lambda p: (x_i * z_size + p, rep_i)))
    if space_size // z_size > 1:
        levels.append((space_size // z_size, x_i, lambda p: (p * z_size + z_i, rep_i)))
    return levels


def reduce_kernel(
    space_size, rep_size, tbl_ref, x_ref, g_ref, cot_ref, occ_ref, wt_ref, o_ref, in_grad_ref, *scratch,
):
    levels = sum_levels(space_size, rep_size)
    count = len(levels)
    buf, full, col_ref, send_sem, recv_sem, local_sem = scratch[:6]
    recvs = scratch[6:]
    rows = buf.shape[0]
    slots, channels, voxels = cot_ref.shape
    edges = edge_masks((1, voxels))
    windows = 2 * count - 1
    mesh_ids = pl.DeviceIdType.MESH

    def bricks_of(window):
        for brick in range(window, slots, windows):
            backward_brick(tbl_ref, g_ref, cot_ref, occ_ref, wt_ref, in_grad_ref, col_ref, edges, brick)

    barrier = pltpu.get_barrier_semaphore()
    for n, r, device in levels:
        for d in range(1, n):
            pl.semaphore_signal(barrier, 1, device_id=device((r + d) % n), device_id_type=mesh_ids)
    pl.semaphore_wait(barrier, sum(n - 1 for n, _, _ in levels))
    first = pltpu.make_async_copy(x_ref, buf, local_sem)
    first.start()
    first.wait()
    lo = 0
    length = rows
    for i, (n, r, device) in enumerate(levels[:-1]):
        chunk = length // n
        copies = []
        for d in range(1, n):
            p = (r + d) % n
            copy = pltpu.make_async_remote_copy(
                src_ref=buf.at[pl.ds(pl.multiple_of(lo + p * chunk, 8), chunk)],
                dst_ref=recvs[i].at[d],
                send_sem=send_sem.at[i, d],
                recv_sem=recv_sem.at[i, d],
                device_id=device(p),
                device_id_type=mesh_ids,
            )
            copy.start()
            copies.append(copy)
        bricks_of(i)
        for copy in copies:
            copy.wait()
        mine = pl.multiple_of(lo + r * chunk, 8)
        total = buf[pl.ds(mine, chunk)]
        for d in range(1, n):
            total = total + recvs[i][d]
        buf[pl.ds(mine, chunk)] = total
        lo = mine
        length = chunk
    last = count - 1
    n, r, device = levels[last]
    stage = recvs[last]
    stage[0] = buf[pl.ds(lo, length)]
    copies = []
    for d in range(1, n):
        copy = pltpu.make_async_remote_copy(
            src_ref=buf.at[pl.ds(lo, length)],
            dst_ref=stage.at[d],
            send_sem=send_sem.at[last, d],
            recv_sem=recv_sem.at[last, d],
            device_id=device((r + d) % n),
            device_id_type=mesh_ids,
        )
        copy.start()
        copies.append(copy)
    bricks_of(last)
    for copy in copies:
        copy.wait()
    total = stage[(r + n) % n]
    for m in range(1, n):
        total = total + stage[(r + n - m) % n]
    full[pl.ds(lo, length)] = total
    for i in reversed(range(last)):
        n, r, device = levels[i]
        copies = []
        for d in range(1, n):
            copy = pltpu.make_async_remote_copy(
                src_ref=full.at[pl.ds(lo, length)],
                dst_ref=full.at[pl.ds(lo, length)],
                send_sem=send_sem.at[count + i, d],
                recv_sem=recv_sem.at[count + i, d],
                device_id=device((r + d) % n),
                device_id_type=mesh_ids,
            )
            copy.start()
            copies.append(copy)
        bricks_of(2 * count - 1 - 1 - i)
        for copy in copies:
            copy.wait()
        lo = pl.multiple_of(lo - r * length, 8)
        length = n * length
    o_ref[...] = full[...]


def all_sum_and_backward(weight_terms, bias_terms, tbl, grad_table, incoming, keep_float, w_t):
    flat = jnp.concatenate([weight_terms.reshape(-1), bias_terms])
    space_size = lax.axis_size("space")
    rep_size = lax.axis_size("rep")
    z_size = 8 if space_size % 8 == 0 else space_size
    sizes = [n for n in (rep_size, z_size, space_size // z_size) if n > 1]
    unit = 8 * math.prod(sizes[:-1])
    whole = flat.shape[0]
    rows = -(-(-(-whole // 128)) // unit) * unit
    x = jnp.pad(flat, (0, rows * 128 - whole)).reshape(rows, 128)
    recvs = []
    length = rows
    for n in sizes[:-1]:
        length //= n
        recvs.append(pltpu.VMEM((n, length, 128), jnp.float32))
    recvs.append(pltpu.VMEM((sizes[-1], length, 128), jnp.float32))
    slots, channels, voxels = incoming.shape
    summed, in_grad = pl.pallas_call(
        functools.partial(reduce_kernel, space_size, rep_size),
        out_shape=(
            jax.ShapeDtypeStruct((rows, 128), jnp.float32),
            jax.ShapeDtypeStruct((slots, channels, voxels), jnp.bfloat16),
        ),
        in_specs=[pl.BlockSpec(memory_space=pltpu.SMEM)] + vmem_specs(5),
        out_specs=tuple(vmem_specs(2)),
        scratch_shapes=[
            pltpu.VMEM((rows, 128), jnp.float32),
            pltpu.VMEM((rows, 128), jnp.float32),
            pltpu.VMEM((27 * channels, voxels), jnp.bfloat16),
            pltpu.SemaphoreType.DMA((2 * len(sizes), max(sizes))),
            pltpu.SemaphoreType.DMA((2 * len(sizes), max(sizes))),
            pltpu.SemaphoreType.DMA(()),
        ]
        + recvs,
        compiler_params=pltpu.CompilerParams(collective_id=0, has_side_effects=True),
        interpret=REMOTE_INTERPRET,
    )(tbl, x, grad_table, incoming, keep_float, w_t)
    x = summed.reshape(-1)[:whole]
    return x[: weight_terms.size].reshape(weight_terms.shape), x[weight_terms.size :], in_grad


def on_device(feats, cotangent, weight, bias, neighbours, occupancy):
    filled = occupancy[0]
    incoming = cotangent[0]
    slot_count, channels = (feats.shape[1], feats.shape[2])
    my_index = lax.axis_index("space")
    masked = feats[0] * filled.astype(jnp.bfloat16)[:, None, :]
    keep_float = filled.astype(jnp.float32)[:, None, :]
    tbl = slot_table(neighbours[0], my_index)
    w_all = weight.transpose(1, 0, 2).reshape(channels, 27 * channels)
    w_t = weight.transpose(2, 0, 1).reshape(channels, 27 * channels)
    result, grad_pre, dw, db = run_forward(
        tbl, exchange_planes(masked), incoming, keep_float, w_all, bias.reshape(channels, 1)
    )
    weight_terms = dw.reshape(channels, 27, channels).transpose(1, 0, 2)
    weight_total, bias_total, in_grad = all_sum_and_backward(
        weight_terms, db.reshape(channels), tbl, exchange_planes(grad_pre), incoming, keep_float, w_t
    )
    normaliser = 1.0 / math.sqrt(
        feats.shape[0] * lax.axis_size("rep") * slot_count * lax.axis_size("space") * 512
    )
    return (result[None], in_grad[None], weight_total * normaliser, bias_total * normaliser)


def solution(mesh):
    placed = (
        P("rep", "space", None, None),
        P("rep", "space", None, None),
        P(),
        P(),
        P("rep", "space", None),
        P("rep", "space", None),
    )
    return jax.shard_map(
        on_device,
        mesh=mesh,
        in_specs=placed,
        out_specs=(P("rep", "space", None, None), P("rep", "space", None, None), P(), P()),
        check_vma=False,
    )
```

```python
import functools
import math

import jax
import jax.numpy as jnp
from jax import lax
from jax.experimental import pallas as pl
from jax.experimental.pallas import tpu as pltpu
from jax.sharding import PartitionSpec as P

INTERPRET = False
REMOTE_INTERPRET = False

DIRECTIONS = [
    (a, b, c) for a in (-1, 0, 1) for b in (-1, 0, 1) for c in (-1, 0, 1) if (a, b, c) != (0, 0, 0)
]
OFFSETS = [(a - 1, b - 1, c - 1) for a in range(3) for b in range(3) for c in range(3)]
STRIDES = (64, 8, 1)
ZERO_SLOT = 12


def offset_terms(shift):
    moving = [axis for axis in range(3) if shift[axis] != 0]
    terms = []
    for pick in range(1 << len(moving)):
        out_axes = [axis for n, axis in enumerate(moving) if (pick >> n) & 1]
        direction = tuple(shift[axis] if axis in out_axes else 0 for axis in range(3))
        flat = sum(STRIDES[axis] * (shift[axis] - (8 * shift[axis] if axis in out_axes else 0)) for axis in range(3))
        pattern = [(axis, shift[axis], axis in out_axes) for axis in moving]
        terms.append((direction, (-flat) % 512, pattern))
    return terms


def gather_columns(src_ref, tbl_ref, brick, col_ref, sign, edges):
    base = brick * 26
    for k, off in enumerate(OFFSETS):
        shift = tuple(sign * s for s in off)
        val = None
        for direction, roll, pattern in offset_terms(shift):
            if direction == (0, 0, 0):
                field = src_ref[brick]
            else:
                slot = tbl_ref[base + DIRECTIONS.index(direction)]
                field = src_ref[slot]
            if roll:
                field = pltpu.roll(field, roll, 1)
            if val is None:
                val = field
                continue
            mask = None
            for axis, step, out in pattern:
                m = edges[(axis, step)] if out else jnp.logical_not(edges[(axis, step)])
                mask = m if mask is None else jnp.logical_and(mask, m)
            val = jnp.where(mask, field, val)
        col_ref[pl.ds(k * 64, 64), :] = val


def edge_masks(shape):
    v = lax.broadcasted_iota(jnp.int32, shape, 1)
    coords = (v >> 6, (v >> 3) & 7, v & 7)
    edges = {}
    for axis in range(3):
        edges[(axis, -1)] = coords[axis] == 0
        edges[(axis, 1)] = coords[axis] == 7
    return edges


def forward_kernel(tbl_ref, x_ref, cot_ref, occ_ref, w_ref, bias_ref, out_ref, gp_ref, dw_ref, db_ref, col_ref):
    slots, channels, voxels = cot_ref.shape
    edges = edge_masks((1, voxels))
    dw_ref[...] = jnp.zeros_like(dw_ref)
    db_ref[...] = jnp.zeros_like(db_ref)

    def brick_step(brick, carry):
        gather_columns(x_ref, tbl_ref, brick, col_ref, 1, edges)
        pre = jnp.dot(w_ref[...], col_ref[...], preferred_element_type=jnp.float32) + bias_ref[...]
        sig = 1.0 / (1.0 + jnp.exp(-pre))
        keep = occ_ref[brick]
        masked = x_ref[brick].astype(jnp.float32)
        out_ref[brick] = (masked + keep * pre * sig).astype(out_ref.dtype)
        gp = (cot_ref[brick].astype(jnp.float32) * keep * sig * (1.0 + pre * (1.0 - sig))).astype(jnp.bfloat16)
        gp_ref[brick] = gp
        dw_ref[...] += lax.dot_general(
            gp, col_ref[...], (((1,), (1,)), ((), ())), preferred_element_type=jnp.float32
        )
        db_ref[...] += jnp.sum(gp.astype(jnp.float32), axis=1, keepdims=True)
        return carry

    lax.fori_loop(0, slots, brick_step, 0)


def backward_brick(tbl_ref, g_ref, cot_ref, occ_ref, wt_ref, in_grad_ref, col_ref, edges, brick):
    gather_columns(g_ref, tbl_ref, brick, col_ref, -1, edges)
    back = jnp.dot(wt_ref[...], col_ref[...], preferred_element_type=jnp.float32)
    keep = occ_ref[brick]
    in_grad_ref[brick] = (keep * (cot_ref[brick].astype(jnp.float32) + back)).astype(in_grad_ref.dtype)


def vmem_specs(n):
    return [pl.BlockSpec(memory_space=pltpu.VMEM)] * n


def run_forward(tbl, table, cot, occ, w_all, bias):
    slots, channels, voxels = cot.shape
    return pl.pallas_call(
        forward_kernel,
        out_shape=(
            jax.ShapeDtypeStruct((slots, channels, voxels), jnp.bfloat16),
            jax.ShapeDtypeStruct((slots, channels, voxels), jnp.bfloat16),
            jax.ShapeDtypeStruct((channels, 27 * channels), jnp.float32),
            jax.ShapeDtypeStruct((channels, 1), jnp.float32),
        ),
        in_specs=[pl.BlockSpec(memory_space=pltpu.SMEM)] + vmem_specs(5),
        out_specs=tuple(vmem_specs(4)),
        scratch_shapes=[pltpu.VMEM((27 * channels, voxels), jnp.bfloat16)],
        interpret=INTERPRET,
    )(tbl, table, cot, occ, w_all, bias)


def exchange_planes(field):
    size = lax.axis_size("space")
    up = [(i, i + 1) for i in range(size - 1)]
    down = [(i + 1, i) for i in range(size - 1)]
    voxels = field.shape[-1]
    low = field[:, :, :64]
    high = field[:, :, voxels - 64 :]
    from_left = lax.ppermute(high, "space", up)
    from_right = lax.ppermute(low, "space", down)
    left = jnp.pad(from_left, ((0, 0), (0, 0), (voxels - 64, 0)))
    right = jnp.pad(from_right, ((0, 0), (0, 0), (0, voxels - 64)))
    zero = jnp.zeros((1,) + field.shape[1:], field.dtype)
    return jnp.concatenate([field, left, right, zero])


def slot_table(neighbour_ids, my_index):
    slots = neighbour_ids.shape[0]
    dx = jnp.array([d[0] for d in DIRECTIONS], jnp.int32)[None, :]
    local = neighbour_ids - (my_index + dx) * slots
    base = jnp.where(dx == 0, 0, jnp.where(dx < 0, slots, 2 * slots))
    table = jnp.where(neighbour_ids >= 0, base + jnp.clip(local, 0, slots - 1), 3 * slots)
    return table.reshape(-1).astype(jnp.int32)


SUM_AXES = ("space", "rep")


def sum_levels(space_size, rep_size):
    z_size = 8 if space_size % 8 == 0 else space_size
    space_i = lax.axis_index("space")
    rep_i = lax.axis_index("rep")
    x_i, z_i = space_i // z_size, space_i % z_size
    levels = []
    if rep_size > 1:
        levels.append((rep_size, rep_i, lambda p: (space_i, p)))
    if z_size > 1:
        levels.append((z_size, z_i, lambda p: (x_i * z_size + p, rep_i)))
    if space_size // z_size > 1:
        levels.append((space_size // z_size, x_i, lambda p: (p * z_size + z_i, rep_i)))
    return levels


def reduce_kernel(
    space_size, rep_size, tbl_ref, x_ref, gp_ref, cot_ref, occ_ref, wt_ref, o_ref, in_grad_ref, *scratch,
):
    levels = sum_levels(space_size, rep_size)
    count = len(levels)
    buf, full, col_ref, send_sem, recv_sem, local_sem, g_ref, plane_send, plane_recv = scratch[:9]
    recvs = scratch[9:]
    rows = buf.shape[0]
    slots, channels, voxels = cot_ref.shape
    edges = edge_masks((1, voxels))
    windows = 2 * count - 1
    mesh_ids = pl.DeviceIdType.MESH

    def bricks_of(window):
        for brick in range(window, slots, windows):
            backward_brick(tbl_ref, g_ref, cot_ref, occ_ref, wt_ref, in_grad_ref, col_ref, edges, brick)

    space_i = lax.axis_index("space")
    rep_i = lax.axis_index("rep")
    sides = ((space_i + 1) % space_size, (space_i + space_size - 1) % space_size)
    g_ref[pl.ds(slots, 2 * slots + 1)] = jnp.zeros((2 * slots + 1, channels, voxels), g_ref.dtype)
    g_ref[pl.ds(0, slots)] = gp_ref[...]
    barrier = pltpu.get_barrier_semaphore()
    for n, r, device in levels:
        for d in range(1, n):
            pl.semaphore_signal(barrier, 1, device_id=device((r + d) % n), device_id_type=mesh_ids)
    for side in sides:
        pl.semaphore_signal(barrier, 1, device_id=(side, rep_i), device_id_type=mesh_ids)
    pl.semaphore_wait(barrier, sum(n - 1 for n, _, _ in levels) + 2)
    planes = []
    for way, side in enumerate(sides):
        lanes = pl.ds(voxels - 128, 128) if way == 0 else pl.ds(0, 128)
        for brick in range(slots):
            copy = pltpu.make_async_remote_copy(
                src_ref=gp_ref.at[brick, :, lanes],
                dst_ref=g_ref.at[(way + 1) * slots + brick, :, lanes],
                send_sem=plane_send.at[way, brick],
                recv_sem=plane_recv.at[way, brick],
                device_id=(side, rep_i),
                device_id_type=mesh_ids,
            )
            copy.start()
            planes.append(copy)
    first = pltpu.make_async_copy(x_ref, buf, local_sem)
    first.start()
    first.wait()
    lo = 0
    length = rows
    for i, (n, r, device) in enumerate(levels[:-1]):
        chunk = length // n
        copies = []
        for d in range(1, n):
            p = (r + d) % n
            copy = pltpu.make_async_remote_copy(
                src_ref=buf.at[pl.ds(pl.multiple_of(lo + p * chunk, 8), chunk)],
                dst_ref=recvs[i].at[d],
                send_sem=send_sem.at[i, d],
                recv_sem=recv_sem.at[i, d],
                device_id=device(p),
                device_id_type=mesh_ids,
            )
            copy.start()
            copies.append(copy)
        if i == 0:
            for copy in planes:
                copy.wait()
        bricks_of(i)
        for copy in copies:
            copy.wait()
        mine = pl.multiple_of(lo + r * chunk, 8)
        total = buf[pl.ds(mine, chunk)]
        for d in range(1, n):
            total = total + recvs[i][d]
        buf[pl.ds(mine, chunk)] = total
        lo = mine
        length = chunk
    last = count - 1
    n, r, device = levels[last]
    stage = recvs[last]
    stage[0] = buf[pl.ds(lo, length)]
    copies = []
    for d in range(1, n):
        copy = pltpu.make_async_remote_copy(
            src_ref=buf.at[pl.ds(lo, length)],
            dst_ref=stage.at[d],
            send_sem=send_sem.at[last, d],
            recv_sem=recv_sem.at[last, d],
            device_id=device((r + d) % n),
            device_id_type=mesh_ids,
        )
        copy.start()
        copies.append(copy)
    bricks_of(last)
    for copy in copies:
        copy.wait()
    total = stage[(r + n) % n]
    for m in range(1, n):
        total = total + stage[(r + n - m) % n]
    full[pl.ds(lo, length)] = total
    for i in reversed(range(last)):
        n, r, device = levels[i]
        copies = []
        for d in range(1, n):
            copy = pltpu.make_async_remote_copy(
                src_ref=full.at[pl.ds(lo, length)],
                dst_ref=full.at[pl.ds(lo, length)],
                send_sem=send_sem.at[count + i, d],
                recv_sem=recv_sem.at[count + i, d],
                device_id=device((r + d) % n),
                device_id_type=mesh_ids,
            )
            copy.start()
            copies.append(copy)
        bricks_of(2 * count - 1 - 1 - i)
        for copy in copies:
            copy.wait()
        lo = pl.multiple_of(lo - r * length, 8)
        length = n * length
    o_ref[...] = full[...]


def all_sum_and_backward(weight_terms, bias_terms, tbl, grad_pre, incoming, keep_float, w_t):
    flat = jnp.concatenate([weight_terms.reshape(-1), bias_terms])
    space_size = lax.axis_size("space")
    rep_size = lax.axis_size("rep")
    z_size = 8 if space_size % 8 == 0 else space_size
    sizes = [n for n in (rep_size, z_size, space_size // z_size) if n > 1]
    unit = 8 * math.prod(sizes[:-1])
    whole = flat.shape[0]
    rows = -(-(-(-whole // 128)) // unit) * unit
    x = jnp.pad(flat, (0, rows * 128 - whole)).reshape(rows, 128)
    recvs = []
    length = rows
    for n in sizes[:-1]:
        length //= n
        recvs.append(pltpu.VMEM((n, length, 128), jnp.float32))
    recvs.append(pltpu.VMEM((sizes[-1], length, 128), jnp.float32))
    slots, channels, voxels = incoming.shape
    summed, in_grad = pl.pallas_call(
        functools.partial(reduce_kernel, space_size, rep_size),
        out_shape=(
            jax.ShapeDtypeStruct((rows, 128), jnp.float32),
            jax.ShapeDtypeStruct((slots, channels, voxels), jnp.bfloat16),
        ),
        in_specs=[pl.BlockSpec(memory_space=pltpu.SMEM)] + vmem_specs(5),
        out_specs=tuple(vmem_specs(2)),
        scratch_shapes=[
            pltpu.VMEM((rows, 128), jnp.float32),
            pltpu.VMEM((rows, 128), jnp.float32),
            pltpu.VMEM((27 * channels, voxels), jnp.bfloat16),
            pltpu.SemaphoreType.DMA((2 * len(sizes), max(sizes))),
            pltpu.SemaphoreType.DMA((2 * len(sizes), max(sizes))),
            pltpu.SemaphoreType.DMA(()),
            pltpu.VMEM((3 * slots + 1, channels, voxels), jnp.bfloat16),
            pltpu.SemaphoreType.DMA((2, slots)),
            pltpu.SemaphoreType.DMA((2, slots)),
        ]
        + recvs,
        compiler_params=pltpu.CompilerParams(collective_id=0, has_side_effects=True),
        interpret=REMOTE_INTERPRET,
    )(tbl, x, grad_pre, incoming, keep_float, w_t)
    x = summed.reshape(-1)[:whole]
    return x[: weight_terms.size].reshape(weight_terms.shape), x[weight_terms.size :], in_grad


def on_device(feats, cotangent, weight, bias, neighbours, occupancy):
    filled = occupancy[0]
    incoming = cotangent[0]
    slot_count, channels = (feats.shape[1], feats.shape[2])
    my_index = lax.axis_index("space")
    masked = feats[0] * filled.astype(jnp.bfloat16)[:, None, :]
    keep_float = filled.astype(jnp.float32)[:, None, :]
    tbl = slot_table(neighbours[0], my_index)
    w_all = weight.transpose(1, 0, 2).reshape(channels, 27 * channels)
    w_t = weight.transpose(2, 0, 1).reshape(channels, 27 * channels)
    result, grad_pre, dw, db = run_forward(
        tbl, exchange_planes(masked), incoming, keep_float, w_all, bias.reshape(channels, 1)
    )
    weight_terms = dw.reshape(channels, 27, channels).transpose(1, 0, 2)
    weight_total, bias_total, in_grad = all_sum_and_backward(
        weight_terms, db.reshape(channels), tbl, grad_pre, incoming, keep_float, w_t
    )
    normaliser = 1.0 / math.sqrt(
        feats.shape[0] * lax.axis_size("rep") * slot_count * lax.axis_size("space") * 512
    )
    return (result[None], in_grad[None], weight_total * normaliser, bias_total * normaliser)


def solution(mesh):
    placed = (
        P("rep", "space", None, None),
        P("rep", "space", None, None),
        P(),
        P(),
        P("rep", "space", None),
        P("rep", "space", None),
    )
    return jax.shard_map(
        on_device,
        mesh=mesh,
        in_specs=placed,
        out_specs=(P("rep", "space", None, None), P("rep", "space", None, None), P(), P()),
        check_vma=False,
    )
```

```python
import functools
import math

import jax
import jax.numpy as jnp
from jax import lax
from jax.experimental import pallas as pl
from jax.experimental.pallas import tpu as pltpu
from jax.sharding import PartitionSpec as P

INTERPRET = False
REMOTE_INTERPRET = False

DIRECTIONS = [
    (a, b, c) for a in (-1, 0, 1) for b in (-1, 0, 1) for c in (-1, 0, 1) if (a, b, c) != (0, 0, 0)
]
OFFSETS = [(a - 1, b - 1, c - 1) for a in range(3) for b in range(3) for c in range(3)]
STRIDES = (64, 8, 1)
ZERO_SLOT = 12


def offset_terms(shift):
    moving = [axis for axis in range(3) if shift[axis] != 0]
    terms = []
    for pick in range(1 << len(moving)):
        out_axes = [axis for n, axis in enumerate(moving) if (pick >> n) & 1]
        direction = tuple(shift[axis] if axis in out_axes else 0 for axis in range(3))
        flat = sum(STRIDES[axis] * (shift[axis] - (8 * shift[axis] if axis in out_axes else 0)) for axis in range(3))
        pattern = [(axis, shift[axis], axis in out_axes) for axis in moving]
        terms.append((direction, (-flat) % 512, pattern))
    return terms


def gather_columns(src_ref, tbl_ref, brick, col_ref, sign, edges):
    base = brick * 26
    for k, off in enumerate(OFFSETS):
        shift = tuple(sign * s for s in off)
        val = None
        for direction, roll, pattern in offset_terms(shift):
            if direction == (0, 0, 0):
                field = src_ref[brick]
            else:
                slot = tbl_ref[base + DIRECTIONS.index(direction)]
                field = src_ref[slot]
            if roll:
                field = pltpu.roll(field, roll, 1)
            if val is None:
                val = field
                continue
            mask = None
            for axis, step, out in pattern:
                m = edges[(axis, step)] if out else jnp.logical_not(edges[(axis, step)])
                mask = m if mask is None else jnp.logical_and(mask, m)
            val = jnp.where(mask, field, val)
        col_ref[pl.ds(k * 64, 64), :] = val


def edge_masks(shape):
    v = lax.broadcasted_iota(jnp.int32, shape, 1)
    coords = (v >> 6, (v >> 3) & 7, v & 7)
    edges = {}
    for axis in range(3):
        edges[(axis, -1)] = coords[axis] == 0
        edges[(axis, 1)] = coords[axis] == 7
    return edges


def forward_kernel(
    space_size, tbl_ref, xm_ref, cot_ref, occ_ref, w_ref, bias_ref, out_ref, gp_ref, dw_ref, db_ref,
    col_ref, x_ref, plane_send, plane_recv,
):
    slots, channels, voxels = cot_ref.shape
    edges = edge_masks((1, voxels))
    space_i = lax.axis_index("space")
    rep_i = lax.axis_index("rep")
    mesh_ids = pl.DeviceIdType.MESH
    sides = ((space_i + 1) % space_size, (space_i + space_size - 1) % space_size)
    x_ref[pl.ds(slots, 2 * slots + 1)] = jnp.zeros((2 * slots + 1, channels, voxels), x_ref.dtype)
    x_ref[pl.ds(0, slots)] = xm_ref[...]
    barrier = pltpu.get_barrier_semaphore()
    for side in sides:
        pl.semaphore_signal(barrier, 1, device_id=(side, rep_i), device_id_type=mesh_ids)
    pl.semaphore_wait(barrier, 2)
    planes = []
    for way, side in enumerate(sides):
        lanes = pl.ds(voxels - 128, 128) if way == 0 else pl.ds(0, 128)
        for brick in range(slots):
            copy = pltpu.make_async_remote_copy(
                src_ref=xm_ref.at[brick, :, lanes],
                dst_ref=x_ref.at[(way + 1) * slots + brick, :, lanes],
                send_sem=plane_send.at[way, brick],
                recv_sem=plane_recv.at[way, brick],
                device_id=(side, rep_i),
                device_id_type=mesh_ids,
            )
            copy.start()
            planes.append(copy)
    for copy in planes:
        copy.wait()
    dw_ref[...] = jnp.zeros_like(dw_ref)
    db_ref[...] = jnp.zeros_like(db_ref)

    def brick_step(brick, carry):
        gather_columns(x_ref, tbl_ref, brick, col_ref, 1, edges)
        pre = jnp.dot(w_ref[...], col_ref[...], preferred_element_type=jnp.float32) + bias_ref[...]
        sig = 1.0 / (1.0 + jnp.exp(-pre))
        keep = occ_ref[brick]
        masked = x_ref[brick].astype(jnp.float32)
        out_ref[brick] = (masked + keep * pre * sig).astype(out_ref.dtype)
        gp = (cot_ref[brick].astype(jnp.float32) * keep * sig * (1.0 + pre * (1.0 - sig))).astype(jnp.bfloat16)
        gp_ref[brick] = gp
        dw_ref[...] += lax.dot_general(
            gp, col_ref[...], (((1,), (1,)), ((), ())), preferred_element_type=jnp.float32
        )
        db_ref[...] += jnp.sum(gp.astype(jnp.float32), axis=1, keepdims=True)
        return carry

    lax.fori_loop(0, slots, brick_step, 0)


def backward_brick(tbl_ref, g_ref, cot_ref, occ_ref, wt_ref, in_grad_ref, col_ref, edges, brick):
    gather_columns(g_ref, tbl_ref, brick, col_ref, -1, edges)
    back = jnp.dot(wt_ref[...], col_ref[...], preferred_element_type=jnp.float32)
    keep = occ_ref[brick]
    in_grad_ref[brick] = (keep * (cot_ref[brick].astype(jnp.float32) + back)).astype(in_grad_ref.dtype)


def vmem_specs(n):
    return [pl.BlockSpec(memory_space=pltpu.VMEM)] * n


def run_forward(tbl, masked, cot, occ, w_all, bias):
    slots, channels, voxels = cot.shape
    return pl.pallas_call(
        functools.partial(forward_kernel, lax.axis_size("space")),
        out_shape=(
            jax.ShapeDtypeStruct((slots, channels, voxels), jnp.bfloat16),
            jax.ShapeDtypeStruct((slots, channels, voxels), jnp.bfloat16),
            jax.ShapeDtypeStruct((channels, 27 * channels), jnp.float32),
            jax.ShapeDtypeStruct((channels, 1), jnp.float32),
        ),
        in_specs=[pl.BlockSpec(memory_space=pltpu.SMEM)] + vmem_specs(5),
        out_specs=tuple(vmem_specs(4)),
        scratch_shapes=[
            pltpu.VMEM((27 * channels, voxels), jnp.bfloat16),
            pltpu.VMEM((3 * slots + 1, channels, voxels), jnp.bfloat16),
            pltpu.SemaphoreType.DMA((2, slots)),
            pltpu.SemaphoreType.DMA((2, slots)),
        ],
        compiler_params=pltpu.CompilerParams(collective_id=1, has_side_effects=True),
        interpret=REMOTE_INTERPRET,
    )(tbl, masked, cot, occ, w_all, bias)


def exchange_planes(field):
    size = lax.axis_size("space")
    up = [(i, i + 1) for i in range(size - 1)]
    down = [(i + 1, i) for i in range(size - 1)]
    voxels = field.shape[-1]
    low = field[:, :, :64]
    high = field[:, :, voxels - 64 :]
    from_left = lax.ppermute(high, "space", up)
    from_right = lax.ppermute(low, "space", down)
    left = jnp.pad(from_left, ((0, 0), (0, 0), (voxels - 64, 0)))
    right = jnp.pad(from_right, ((0, 0), (0, 0), (0, voxels - 64)))
    zero = jnp.zeros((1,) + field.shape[1:], field.dtype)
    return jnp.concatenate([field, left, right, zero])


def slot_table(neighbour_ids, my_index):
    slots = neighbour_ids.shape[0]
    dx = jnp.array([d[0] for d in DIRECTIONS], jnp.int32)[None, :]
    local = neighbour_ids - (my_index + dx) * slots
    base = jnp.where(dx == 0, 0, jnp.where(dx < 0, slots, 2 * slots))
    table = jnp.where(neighbour_ids >= 0, base + jnp.clip(local, 0, slots - 1), 3 * slots)
    return table.reshape(-1).astype(jnp.int32)


SUM_AXES = ("space", "rep")


def sum_levels(space_size, rep_size):
    z_size = 8 if space_size % 8 == 0 else space_size
    space_i = lax.axis_index("space")
    rep_i = lax.axis_index("rep")
    x_i, z_i = space_i // z_size, space_i % z_size
    levels = []
    if rep_size > 1:
        levels.append((rep_size, rep_i, lambda p: (space_i, p)))
    if z_size > 1:
        levels.append((z_size, z_i, lambda p: (x_i * z_size + p, rep_i)))
    if space_size // z_size > 1:
        levels.append((space_size // z_size, x_i, lambda p: (p * z_size + z_i, rep_i)))
    return levels


def reduce_kernel(
    space_size, rep_size, tbl_ref, x_ref, gp_ref, cot_ref, occ_ref, wt_ref, o_ref, in_grad_ref, *scratch,
):
    levels = sum_levels(space_size, rep_size)
    count = len(levels)
    buf, full, col_ref, send_sem, recv_sem, local_sem, g_ref, plane_send, plane_recv = scratch[:9]
    recvs = scratch[9:]
    rows = buf.shape[0]
    slots, channels, voxels = cot_ref.shape
    edges = edge_masks((1, voxels))
    windows = 2 * count - 1
    mesh_ids = pl.DeviceIdType.MESH

    def bricks_of(window):
        for brick in range(window, slots, windows):
            backward_brick(tbl_ref, g_ref, cot_ref, occ_ref, wt_ref, in_grad_ref, col_ref, edges, brick)

    space_i = lax.axis_index("space")
    rep_i = lax.axis_index("rep")
    sides = ((space_i + 1) % space_size, (space_i + space_size - 1) % space_size)
    g_ref[pl.ds(slots, 2 * slots + 1)] = jnp.zeros((2 * slots + 1, channels, voxels), g_ref.dtype)
    g_ref[pl.ds(0, slots)] = gp_ref[...]
    barrier = pltpu.get_barrier_semaphore()
    for n, r, device in levels:
        for d in range(1, n):
            pl.semaphore_signal(barrier, 1, device_id=device((r + d) % n), device_id_type=mesh_ids)
    for side in sides:
        pl.semaphore_signal(barrier, 1, device_id=(side, rep_i), device_id_type=mesh_ids)
    pl.semaphore_wait(barrier, sum(n - 1 for n, _, _ in levels) + 2)
    planes = []
    for way, side in enumerate(sides):
        lanes = pl.ds(voxels - 128, 128) if way == 0 else pl.ds(0, 128)
        for brick in range(slots):
            copy = pltpu.make_async_remote_copy(
                src_ref=gp_ref.at[brick, :, lanes],
                dst_ref=g_ref.at[(way + 1) * slots + brick, :, lanes],
                send_sem=plane_send.at[way, brick],
                recv_sem=plane_recv.at[way, brick],
                device_id=(side, rep_i),
                device_id_type=mesh_ids,
            )
            copy.start()
            planes.append(copy)
    first = pltpu.make_async_copy(x_ref, buf, local_sem)
    first.start()
    first.wait()
    lo = 0
    length = rows
    for i, (n, r, device) in enumerate(levels[:-1]):
        chunk = length // n
        copies = []
        for d in range(1, n):
            p = (r + d) % n
            copy = pltpu.make_async_remote_copy(
                src_ref=buf.at[pl.ds(pl.multiple_of(lo + p * chunk, 8), chunk)],
                dst_ref=recvs[i].at[d],
                send_sem=send_sem.at[i, d],
                recv_sem=recv_sem.at[i, d],
                device_id=device(p),
                device_id_type=mesh_ids,
            )
            copy.start()
            copies.append(copy)
        if i == 0:
            for copy in planes:
                copy.wait()
        bricks_of(i)
        for copy in copies:
            copy.wait()
        mine = pl.multiple_of(lo + r * chunk, 8)
        total = buf[pl.ds(mine, chunk)]
        for d in range(1, n):
            total = total + recvs[i][d]
        buf[pl.ds(mine, chunk)] = total
        lo = mine
        length = chunk
    last = count - 1
    n, r, device = levels[last]
    stage = recvs[last]
    stage[0] = buf[pl.ds(lo, length)]
    copies = []
    for d in range(1, n):
        copy = pltpu.make_async_remote_copy(
            src_ref=buf.at[pl.ds(lo, length)],
            dst_ref=stage.at[d],
            send_sem=send_sem.at[last, d],
            recv_sem=recv_sem.at[last, d],
            device_id=device((r + d) % n),
            device_id_type=mesh_ids,
        )
        copy.start()
        copies.append(copy)
    bricks_of(last)
    for copy in copies:
        copy.wait()
    total = stage[(r + n) % n]
    for m in range(1, n):
        total = total + stage[(r + n - m) % n]
    full[pl.ds(lo, length)] = total
    for i in reversed(range(last)):
        n, r, device = levels[i]
        copies = []
        for d in range(1, n):
            copy = pltpu.make_async_remote_copy(
                src_ref=full.at[pl.ds(lo, length)],
                dst_ref=full.at[pl.ds(lo, length)],
                send_sem=send_sem.at[count + i, d],
                recv_sem=recv_sem.at[count + i, d],
                device_id=device((r + d) % n),
                device_id_type=mesh_ids,
            )
            copy.start()
            copies.append(copy)
        bricks_of(2 * count - 1 - 1 - i)
        for copy in copies:
            copy.wait()
        lo = pl.multiple_of(lo - r * length, 8)
        length = n * length
    o_ref[...] = full[...]


def all_sum_and_backward(weight_terms, bias_terms, tbl, grad_pre, incoming, keep_float, w_t):
    flat = jnp.concatenate([weight_terms.reshape(-1), bias_terms])
    space_size = lax.axis_size("space")
    rep_size = lax.axis_size("rep")
    z_size = 8 if space_size % 8 == 0 else space_size
    sizes = [n for n in (rep_size, z_size, space_size // z_size) if n > 1]
    unit = 8 * math.prod(sizes[:-1])
    whole = flat.shape[0]
    rows = -(-(-(-whole // 128)) // unit) * unit
    x = jnp.pad(flat, (0, rows * 128 - whole)).reshape(rows, 128)
    recvs = []
    length = rows
    for n in sizes[:-1]:
        length //= n
        recvs.append(pltpu.VMEM((n, length, 128), jnp.float32))
    recvs.append(pltpu.VMEM((sizes[-1], length, 128), jnp.float32))
    slots, channels, voxels = incoming.shape
    summed, in_grad = pl.pallas_call(
        functools.partial(reduce_kernel, space_size, rep_size),
        out_shape=(
            jax.ShapeDtypeStruct((rows, 128), jnp.float32),
            jax.ShapeDtypeStruct((slots, channels, voxels), jnp.bfloat16),
        ),
        in_specs=[pl.BlockSpec(memory_space=pltpu.SMEM)] + vmem_specs(5),
        out_specs=tuple(vmem_specs(2)),
        scratch_shapes=[
            pltpu.VMEM((rows, 128), jnp.float32),
            pltpu.VMEM((rows, 128), jnp.float32),
            pltpu.VMEM((27 * channels, voxels), jnp.bfloat16),
            pltpu.SemaphoreType.DMA((2 * len(sizes), max(sizes))),
            pltpu.SemaphoreType.DMA((2 * len(sizes), max(sizes))),
            pltpu.SemaphoreType.DMA(()),
            pltpu.VMEM((3 * slots + 1, channels, voxels), jnp.bfloat16),
            pltpu.SemaphoreType.DMA((2, slots)),
            pltpu.SemaphoreType.DMA((2, slots)),
        ]
        + recvs,
        compiler_params=pltpu.CompilerParams(collective_id=0, has_side_effects=True),
        interpret=REMOTE_INTERPRET,
    )(tbl, x, grad_pre, incoming, keep_float, w_t)
    x = summed.reshape(-1)[:whole]
    return x[: weight_terms.size].reshape(weight_terms.shape), x[weight_terms.size :], in_grad


def on_device(feats, cotangent, weight, bias, neighbours, occupancy):
    filled = occupancy[0]
    incoming = cotangent[0]
    slot_count, channels = (feats.shape[1], feats.shape[2])
    my_index = lax.axis_index("space")
    masked = feats[0] * filled.astype(jnp.bfloat16)[:, None, :]
    keep_float = filled.astype(jnp.float32)[:, None, :]
    tbl = slot_table(neighbours[0], my_index)
    w_all = weight.transpose(1, 0, 2).reshape(channels, 27 * channels)
    w_t = weight.transpose(2, 0, 1).reshape(channels, 27 * channels)
    result, grad_pre, dw, db = run_forward(
        tbl, masked, incoming, keep_float, w_all, bias.reshape(channels, 1)
    )
    weight_terms = dw.reshape(channels, 27, channels).transpose(1, 0, 2)
    weight_total, bias_total, in_grad = all_sum_and_backward(
        weight_terms, db.reshape(channels), tbl, grad_pre, incoming, keep_float, w_t
    )
    normaliser = 1.0 / math.sqrt(
        feats.shape[0] * lax.axis_size("rep") * slot_count * lax.axis_size("space") * 512
    )
    return (result[None], in_grad[None], weight_total * normaliser, bias_total * normaliser)


def solution(mesh):
    placed = (
        P("rep", "space", None, None),
        P("rep", "space", None, None),
        P(),
        P(),
        P("rep", "space", None),
        P("rep", "space", None),
    )
    return jax.shard_map(
        on_device,
        mesh=mesh,
        in_specs=placed,
        out_specs=(P("rep", "space", None, None), P("rep", "space", None, None), P(), P()),
        check_vma=False,
    )
```

```python
import functools
import math

import jax
import jax.numpy as jnp
from jax import lax
from jax.experimental import pallas as pl
from jax.experimental.pallas import tpu as pltpu
from jax.sharding import PartitionSpec as P

INTERPRET = False
REMOTE_INTERPRET = False

DIRECTIONS = [
    (a, b, c) for a in (-1, 0, 1) for b in (-1, 0, 1) for c in (-1, 0, 1) if (a, b, c) != (0, 0, 0)
]
OFFSETS = [(a - 1, b - 1, c - 1) for a in range(3) for b in range(3) for c in range(3)]
STRIDES = (64, 8, 1)
ZERO_SLOT = 12


def offset_terms(shift):
    moving = [axis for axis in range(3) if shift[axis] != 0]
    terms = []
    for pick in range(1 << len(moving)):
        out_axes = [axis for n, axis in enumerate(moving) if (pick >> n) & 1]
        direction = tuple(shift[axis] if axis in out_axes else 0 for axis in range(3))
        flat = sum(STRIDES[axis] * (shift[axis] - (8 * shift[axis] if axis in out_axes else 0)) for axis in range(3))
        pattern = [(axis, shift[axis], axis in out_axes) for axis in moving]
        terms.append((direction, (-flat) % 512, pattern))
    return terms


def gather_columns(src_ref, tbl_ref, brick, col_ref, sign, edges):
    base = brick * 26
    for k, off in enumerate(OFFSETS):
        shift = tuple(sign * s for s in off)
        val = None
        for direction, roll, pattern in offset_terms(shift):
            if direction == (0, 0, 0):
                field = src_ref[brick]
            else:
                slot = tbl_ref[base + DIRECTIONS.index(direction)]
                field = src_ref[slot]
            if roll:
                field = pltpu.roll(field, roll, 1)
            if val is None:
                val = field
                continue
            mask = None
            for axis, step, out in pattern:
                m = edges[(axis, step)] if out else jnp.logical_not(edges[(axis, step)])
                mask = m if mask is None else jnp.logical_and(mask, m)
            val = jnp.where(mask, field, val)
        col_ref[pl.ds(k * 64, 64), :] = val


def edge_masks(shape):
    v = lax.broadcasted_iota(jnp.int32, shape, 1)
    coords = (v >> 6, (v >> 3) & 7, v & 7)
    edges = {}
    for axis in range(3):
        edges[(axis, -1)] = coords[axis] == 0
        edges[(axis, 1)] = coords[axis] == 7
    return edges


def forward_kernel(
    space_size, tbl_ref, xm_ref, cot_ref, occ_ref, w_ref, bias_ref, out_ref, gp_ref, dw_ref, db_ref,
    col_ref, x_ref, plane_send, plane_recv,
):
    slots, channels, voxels = cot_ref.shape
    edges = edge_masks((1, voxels))
    space_i = lax.axis_index("space")
    rep_i = lax.axis_index("rep")
    mesh_ids = pl.DeviceIdType.MESH
    sides = ((space_i + 1) % space_size, (space_i + space_size - 1) % space_size)
    x_ref[pl.ds(slots, 2 * slots + 1)] = jnp.zeros((2 * slots + 1, channels, voxels), x_ref.dtype)
    x_ref[pl.ds(0, slots)] = xm_ref[...]
    barrier = pltpu.get_barrier_semaphore()
    for side in sides:
        pl.semaphore_signal(barrier, 1, device_id=(side, rep_i), device_id_type=mesh_ids)
    pl.semaphore_wait(barrier, 2)
    planes = []
    for way, side in enumerate(sides):
        lanes = pl.ds(voxels - 128, 128) if way == 0 else pl.ds(0, 128)
        for brick in range(slots):
            copy = pltpu.make_async_remote_copy(
                src_ref=xm_ref.at[brick, :, lanes],
                dst_ref=x_ref.at[(way + 1) * slots + brick, :, lanes],
                send_sem=plane_send.at[way, brick],
                recv_sem=plane_recv.at[way, brick],
                device_id=(side, rep_i),
                device_id_type=mesh_ids,
            )
            copy.start()
            planes.append(copy)
    for copy in planes:
        copy.wait()
    dw_ref[...] = jnp.zeros_like(dw_ref)
    db_ref[...] = jnp.zeros_like(db_ref)

    def brick_step(brick, carry):
        gather_columns(x_ref, tbl_ref, brick, col_ref, 1, edges)
        pre = jnp.dot(w_ref[...], col_ref[...], preferred_element_type=jnp.float32) + bias_ref[...]
        sig = 1.0 / (1.0 + jnp.exp(-pre))
        keep = occ_ref[brick]
        masked = x_ref[brick].astype(jnp.float32)
        out_ref[brick] = (masked + keep * pre * sig).astype(out_ref.dtype)
        gp = (cot_ref[brick].astype(jnp.float32) * keep * sig * (1.0 + pre * (1.0 - sig))).astype(jnp.bfloat16)
        gp_ref[brick] = gp
        dw_ref[...] += lax.dot_general(
            gp, col_ref[...], (((1,), (1,)), ((), ())), preferred_element_type=jnp.float32
        )
        db_ref[...] += jnp.sum(gp.astype(jnp.float32), axis=1, keepdims=True)
        return carry

    lax.fori_loop(0, slots, brick_step, 0)


def backward_brick(tbl_ref, g_ref, cot_ref, occ_ref, wt_ref, in_grad_ref, col_ref, edges, brick):
    gather_columns(g_ref, tbl_ref, brick, col_ref, -1, edges)
    back = jnp.dot(wt_ref[...], col_ref[...], preferred_element_type=jnp.float32)
    keep = occ_ref[brick]
    in_grad_ref[brick] = (keep * (cot_ref[brick].astype(jnp.float32) + back)).astype(in_grad_ref.dtype)


def vmem_specs(n):
    return [pl.BlockSpec(memory_space=pltpu.VMEM)] * n


def run_forward(tbl, masked, cot, occ, w_all, bias):
    slots, channels, voxels = cot.shape
    return pl.pallas_call(
        functools.partial(forward_kernel, lax.axis_size("space")),
        out_shape=(
            jax.ShapeDtypeStruct((slots, channels, voxels), jnp.bfloat16),
            jax.ShapeDtypeStruct((slots, channels, voxels), jnp.bfloat16),
            jax.ShapeDtypeStruct((channels, 27 * channels), jnp.float32),
            jax.ShapeDtypeStruct((channels, 1), jnp.float32),
        ),
        in_specs=[pl.BlockSpec(memory_space=pltpu.SMEM)] + vmem_specs(5),
        out_specs=tuple(vmem_specs(4)),
        scratch_shapes=[
            pltpu.VMEM((27 * channels, voxels), jnp.bfloat16),
            pltpu.VMEM((3 * slots + 1, channels, voxels), jnp.bfloat16),
            pltpu.SemaphoreType.DMA((2, slots)),
            pltpu.SemaphoreType.DMA((2, slots)),
        ],
        compiler_params=pltpu.CompilerParams(collective_id=1, has_side_effects=True),
        interpret=REMOTE_INTERPRET,
    )(tbl, masked, cot, occ, w_all, bias)


def slot_table(neighbour_ids, my_index):
    slots = neighbour_ids.shape[0]
    dx = jnp.array([d[0] for d in DIRECTIONS], jnp.int32)[None, :]
    local = neighbour_ids - (my_index + dx) * slots
    base = jnp.where(dx == 0, 0, jnp.where(dx < 0, slots, 2 * slots))
    table = jnp.where(neighbour_ids >= 0, base + jnp.clip(local, 0, slots - 1), 3 * slots)
    return table.reshape(-1).astype(jnp.int32)


SUM_AXES = ("space", "rep")


def sum_levels(space_size, rep_size):
    z_size = 8 if space_size % 8 == 0 else space_size
    space_i = lax.axis_index("space")
    rep_i = lax.axis_index("rep")
    x_i, z_i = space_i // z_size, space_i % z_size
    levels = []
    if rep_size > 1:
        levels.append((rep_size, rep_i, lambda p: (space_i, p)))
    if z_size > 1:
        levels.append((z_size, z_i, lambda p: (x_i * z_size + p, rep_i)))
    if space_size // z_size > 1:
        levels.append((space_size // z_size, x_i, lambda p: (p * z_size + z_i, rep_i)))
    return levels


def reduce_kernel(
    space_size, rep_size, tbl_ref, x_ref, gp_ref, cot_ref, occ_ref, wt_ref, o_ref, in_grad_ref, *scratch,
):
    levels = sum_levels(space_size, rep_size)
    count = len(levels)
    buf, full, col_ref, send_sem, recv_sem, local_sem, g_ref, plane_send, plane_recv = scratch[:9]
    recvs = scratch[9:]
    rows = buf.shape[0]
    slots, channels, voxels = cot_ref.shape
    edges = edge_masks((1, voxels))
    windows = 2 * count - 1
    mesh_ids = pl.DeviceIdType.MESH

    def bricks_of(window):
        for brick in range(window, slots, windows):
            backward_brick(tbl_ref, g_ref, cot_ref, occ_ref, wt_ref, in_grad_ref, col_ref, edges, brick)

    space_i = lax.axis_index("space")
    rep_i = lax.axis_index("rep")
    sides = ((space_i + 1) % space_size, (space_i + space_size - 1) % space_size)
    g_ref[pl.ds(slots, 2 * slots + 1)] = jnp.zeros((2 * slots + 1, channels, voxels), g_ref.dtype)
    g_ref[pl.ds(0, slots)] = gp_ref[...]
    barrier = pltpu.get_barrier_semaphore()
    for n, r, device in levels:
        for d in range(1, n):
            pl.semaphore_signal(barrier, 1, device_id=device((r + d) % n), device_id_type=mesh_ids)
    for side in sides:
        pl.semaphore_signal(barrier, 1, device_id=(side, rep_i), device_id_type=mesh_ids)
    pl.semaphore_wait(barrier, sum(n - 1 for n, _, _ in levels) + 2)
    planes = []
    for way, side in enumerate(sides):
        lanes = pl.ds(voxels - 128, 128) if way == 0 else pl.ds(0, 128)
        for brick in range(slots):
            copy = pltpu.make_async_remote_copy(
                src_ref=gp_ref.at[brick, :, lanes],
                dst_ref=g_ref.at[(way + 1) * slots + brick, :, lanes],
                send_sem=plane_send.at[way, brick],
                recv_sem=plane_recv.at[way, brick],
                device_id=(side, rep_i),
                device_id_type=mesh_ids,
            )
            copy.start()
            planes.append(copy)
    first = pltpu.make_async_copy(x_ref, buf, local_sem)
    first.start()
    first.wait()
    lo = 0
    length = rows
    for i, (n, r, device) in enumerate(levels[:-1]):
        chunk = length // n
        copies = []
        for d in range(1, n):
            p = (r + d) % n
            copy = pltpu.make_async_remote_copy(
                src_ref=buf.at[pl.ds(pl.multiple_of(lo + p * chunk, 8), chunk)],
                dst_ref=recvs[i].at[d],
                send_sem=send_sem.at[i, d],
                recv_sem=recv_sem.at[i, d],
                device_id=device(p),
                device_id_type=mesh_ids,
            )
            copy.start()
            copies.append(copy)
        if i == 0:
            for copy in planes:
                copy.wait()
        bricks_of(i)
        for copy in copies:
            copy.wait()
        mine = pl.multiple_of(lo + r * chunk, 8)
        total = buf[pl.ds(mine, chunk)]
        for d in range(1, n):
            total = total + recvs[i][d]
        buf[pl.ds(mine, chunk)] = total
        lo = mine
        length = chunk
    last = count - 1
    n, r, device = levels[last]
    stage = recvs[last]
    stage[0] = buf[pl.ds(lo, length)]
    copies = []
    for d in range(1, n):
        copy = pltpu.make_async_remote_copy(
            src_ref=buf.at[pl.ds(lo, length)],
            dst_ref=stage.at[d],
            send_sem=send_sem.at[last, d],
            recv_sem=recv_sem.at[last, d],
            device_id=device((r + d) % n),
            device_id_type=mesh_ids,
        )
        copy.start()
        copies.append(copy)
    bricks_of(last)
    for copy in copies:
        copy.wait()
    total = stage[(r + n) % n]
    for m in range(1, n):
        total = total + stage[(r + n - m) % n]
    full[pl.ds(lo, length)] = total
    for i in reversed(range(last)):
        n, r, device = levels[i]
        copies = []
        for d in range(1, n):
            copy = pltpu.make_async_remote_copy(
                src_ref=full.at[pl.ds(lo, length)],
                dst_ref=full.at[pl.ds(lo, length)],
                send_sem=send_sem.at[count + i, d],
                recv_sem=recv_sem.at[count + i, d],
                device_id=device((r + d) % n),
                device_id_type=mesh_ids,
            )
            copy.start()
            copies.append(copy)
        bricks_of(2 * count - 1 - 1 - i)
        for copy in copies:
            copy.wait()
        lo = pl.multiple_of(lo - r * length, 8)
        length = n * length
    o_ref[...] = full[...]


def all_sum_and_backward(weight_terms, bias_terms, tbl, grad_pre, incoming, keep_float, w_t):
    flat = jnp.concatenate([weight_terms.reshape(-1), bias_terms])
    space_size = lax.axis_size("space")
    rep_size = lax.axis_size("rep")
    z_size = 8 if space_size % 8 == 0 else space_size
    sizes = [n for n in (rep_size, z_size, space_size // z_size) if n > 1]
    unit = 8 * math.prod(sizes[:-1])
    whole = flat.shape[0]
    rows = -(-(-(-whole // 128)) // unit) * unit
    x = jnp.pad(flat, (0, rows * 128 - whole)).reshape(rows, 128)
    recvs = []
    length = rows
    for n in sizes[:-1]:
        length //= n
        recvs.append(pltpu.VMEM((n, length, 128), jnp.float32))
    recvs.append(pltpu.VMEM((sizes[-1], length, 128), jnp.float32))
    slots, channels, voxels = incoming.shape
    summed, in_grad = pl.pallas_call(
        functools.partial(reduce_kernel, space_size, rep_size),
        out_shape=(
            jax.ShapeDtypeStruct((rows, 128), jnp.float32),
            jax.ShapeDtypeStruct((slots, channels, voxels), jnp.bfloat16),
        ),
        in_specs=[pl.BlockSpec(memory_space=pltpu.SMEM)] + vmem_specs(5),
        out_specs=tuple(vmem_specs(2)),
        scratch_shapes=[
            pltpu.VMEM((rows, 128), jnp.float32),
            pltpu.VMEM((rows, 128), jnp.float32),
            pltpu.VMEM((27 * channels, voxels), jnp.bfloat16),
            pltpu.SemaphoreType.DMA((2 * len(sizes), max(sizes))),
            pltpu.SemaphoreType.DMA((2 * len(sizes), max(sizes))),
            pltpu.SemaphoreType.DMA(()),
            pltpu.VMEM((3 * slots + 1, channels, voxels), jnp.bfloat16),
            pltpu.SemaphoreType.DMA((2, slots)),
            pltpu.SemaphoreType.DMA((2, slots)),
        ]
        + recvs,
        compiler_params=pltpu.CompilerParams(collective_id=0, has_side_effects=True),
        interpret=REMOTE_INTERPRET,
    )(tbl, x, grad_pre, incoming, keep_float, w_t)
    x = summed.reshape(-1)[:whole]
    return x[: weight_terms.size].reshape(weight_terms.shape), x[weight_terms.size :], in_grad


def on_device(feats, cotangent, weight, bias, neighbours, occupancy):
    filled = occupancy[0]
    incoming = cotangent[0]
    slot_count, channels = (feats.shape[1], feats.shape[2])
    my_index = lax.axis_index("space")
    masked = feats[0] * filled.astype(jnp.bfloat16)[:, None, :]
    keep_float = filled.astype(jnp.float32)[:, None, :]
    tbl = slot_table(neighbours[0], my_index)
    w_all = weight.transpose(1, 0, 2).reshape(channels, 27 * channels)
    w_t = weight.transpose(2, 0, 1).reshape(channels, 27 * channels)
    result, grad_pre, dw, db = run_forward(
        tbl, masked, incoming, keep_float, w_all, bias.reshape(channels, 1)
    )
    weight_total, bias_total, in_grad = all_sum_and_backward(
        dw, db.reshape(channels), tbl, grad_pre, incoming, keep_float, w_t
    )
    weight_total = weight_total.reshape(channels, 27, channels).transpose(1, 0, 2)
    normaliser = 1.0 / math.sqrt(
        feats.shape[0] * lax.axis_size("rep") * slot_count * lax.axis_size("space") * 512
    )
    return (result[None], in_grad[None], weight_total * normaliser, bias_total * normaliser)


def solution(mesh):
    placed = (
        P("rep", "space", None, None),
        P("rep", "space", None, None),
        P(),
        P(),
        P("rep", "space", None),
        P("rep", "space", None),
    )
    return jax.shard_map(
        on_device,
        mesh=mesh,
        in_specs=placed,
        out_specs=(P("rep", "space", None, None), P("rep", "space", None, None), P(), P()),
        check_vma=False,
    )
```

```python
import functools
import math

import jax
import jax.numpy as jnp
from jax import lax
from jax.experimental import pallas as pl
from jax.experimental.pallas import tpu as pltpu
from jax.sharding import PartitionSpec as P

INTERPRET = False
REMOTE_INTERPRET = False

DIRECTIONS = [
    (a, b, c) for a in (-1, 0, 1) for b in (-1, 0, 1) for c in (-1, 0, 1) if (a, b, c) != (0, 0, 0)
]
OFFSETS = [(a - 1, b - 1, c - 1) for a in range(3) for b in range(3) for c in range(3)]
STRIDES = (64, 8, 1)
ZERO_SLOT = 12


def offset_terms(shift):
    moving = [axis for axis in range(3) if shift[axis] != 0]
    terms = []
    for pick in range(1 << len(moving)):
        out_axes = [axis for n, axis in enumerate(moving) if (pick >> n) & 1]
        direction = tuple(shift[axis] if axis in out_axes else 0 for axis in range(3))
        flat = sum(STRIDES[axis] * (shift[axis] - (8 * shift[axis] if axis in out_axes else 0)) for axis in range(3))
        pattern = [(axis, shift[axis], axis in out_axes) for axis in moving]
        terms.append((direction, (-flat) % 512, pattern))
    return terms


def gather_columns(src_ref, tbl_ref, brick, col_ref, sign, edges):
    base = brick * 26
    for k, off in enumerate(OFFSETS):
        shift = tuple(sign * s for s in off)
        val = None
        for direction, roll, pattern in offset_terms(shift):
            if direction == (0, 0, 0):
                field = src_ref[brick]
            else:
                slot = tbl_ref[base + DIRECTIONS.index(direction)]
                field = src_ref[slot]
            if roll:
                field = pltpu.roll(field, roll, 1)
            if val is None:
                val = field
                continue
            mask = None
            for axis, step, out in pattern:
                m = edges[(axis, step)] if out else jnp.logical_not(edges[(axis, step)])
                mask = m if mask is None else jnp.logical_and(mask, m)
            val = jnp.where(mask, field, val)
        col_ref[pl.ds(k * 64, 64), :] = val


def edge_masks(shape):
    v = lax.broadcasted_iota(jnp.int32, shape, 1)
    coords = (v >> 6, (v >> 3) & 7, v & 7)
    edges = {}
    for axis in range(3):
        edges[(axis, -1)] = coords[axis] == 0
        edges[(axis, 1)] = coords[axis] == 7
    return edges


def forward_kernel(
    space_size, tbl_ref, xm_ref, cot_ref, occ_ref, w_ref, bias_ref, out_ref, gp_ref, dw_ref, db_ref,
    col_ref, x_ref, plane_send, plane_recv,
):
    slots, channels, voxels = cot_ref.shape
    edges = edge_masks((1, voxels))
    space_i = lax.axis_index("space")
    rep_i = lax.axis_index("rep")
    mesh_ids = pl.DeviceIdType.MESH
    sides = ((space_i + 1) % space_size, (space_i + space_size - 1) % space_size)
    x_ref[pl.ds(slots, 2 * slots + 1)] = jnp.zeros((2 * slots + 1, channels, voxels), x_ref.dtype)
    x_ref[pl.ds(0, slots)] = xm_ref[...]
    barrier = pltpu.get_barrier_semaphore()
    for side in sides:
        pl.semaphore_signal(barrier, 1, device_id=(side, rep_i), device_id_type=mesh_ids)
    pl.semaphore_wait(barrier, 2)
    planes = []
    for way, side in enumerate(sides):
        lanes = pl.ds(voxels - 128, 128) if way == 0 else pl.ds(0, 128)
        for brick in range(slots):
            copy = pltpu.make_async_remote_copy(
                src_ref=xm_ref.at[brick, :, lanes],
                dst_ref=x_ref.at[(way + 1) * slots + brick, :, lanes],
                send_sem=plane_send.at[way, brick],
                recv_sem=plane_recv.at[way, brick],
                device_id=(side, rep_i),
                device_id_type=mesh_ids,
            )
            copy.start()
            planes.append(copy)
    for copy in planes:
        copy.wait()
    dw_ref[...] = jnp.zeros_like(dw_ref)
    db_ref[...] = jnp.zeros_like(db_ref)

    def brick_step(brick, carry):
        gather_columns(x_ref, tbl_ref, brick, col_ref, 1, edges)
        pre = jnp.dot(w_ref[...], col_ref[...], preferred_element_type=jnp.float32) + bias_ref[...]
        sig = 1.0 / (1.0 + jnp.exp(-pre))
        keep = occ_ref[brick]
        masked = x_ref[brick].astype(jnp.float32)
        out_ref[brick] = (masked + keep * pre * sig).astype(out_ref.dtype)
        gp = (cot_ref[brick].astype(jnp.float32) * keep * sig * (1.0 + pre * (1.0 - sig))).astype(jnp.bfloat16)
        gp_ref[brick] = gp
        dw_ref[...] += lax.dot_general(
            gp, col_ref[...], (((1,), (1,)), ((), ())), preferred_element_type=jnp.float32
        )
        db_ref[...] += jnp.sum(gp.astype(jnp.float32), axis=1, keepdims=True)
        return carry

    lax.fori_loop(0, slots, brick_step, 0)


def backward_brick(tbl_ref, g_ref, cot_ref, occ_ref, wt_ref, in_grad_ref, col_ref, edges, brick):
    gather_columns(g_ref, tbl_ref, brick, col_ref, -1, edges)
    back = jnp.dot(wt_ref[...], col_ref[...], preferred_element_type=jnp.float32)
    keep = occ_ref[brick]
    in_grad_ref[brick] = (keep * (cot_ref[brick].astype(jnp.float32) + back)).astype(in_grad_ref.dtype)


def vmem_specs(n):
    return [pl.BlockSpec(memory_space=pltpu.VMEM)] * n


def run_forward(tbl, masked, cot, occ, w_all, bias):
    slots, channels, voxels = cot.shape
    return pl.pallas_call(
        functools.partial(forward_kernel, lax.axis_size("space")),
        out_shape=(
            jax.ShapeDtypeStruct((slots, channels, voxels), jnp.bfloat16),
            jax.ShapeDtypeStruct((slots, channels, voxels), jnp.bfloat16),
            jax.ShapeDtypeStruct((channels, 27 * channels), jnp.float32),
            jax.ShapeDtypeStruct((channels, 1), jnp.float32),
        ),
        in_specs=[pl.BlockSpec(memory_space=pltpu.SMEM)] + vmem_specs(5),
        out_specs=tuple(vmem_specs(4)),
        scratch_shapes=[
            pltpu.VMEM((27 * channels, voxels), jnp.bfloat16),
            pltpu.VMEM((3 * slots + 1, channels, voxels), jnp.bfloat16),
            pltpu.SemaphoreType.DMA((2, slots)),
            pltpu.SemaphoreType.DMA((2, slots)),
        ],
        compiler_params=pltpu.CompilerParams(collective_id=1, has_side_effects=True),
        interpret=REMOTE_INTERPRET,
    )(tbl, masked, cot, occ, w_all, bias)


def exchange_planes(field):
    size = lax.axis_size("space")
    up = [(i, i + 1) for i in range(size - 1)]
    down = [(i + 1, i) for i in range(size - 1)]
    voxels = field.shape[-1]
    low = field[:, :, :64]
    high = field[:, :, voxels - 64 :]
    from_left = lax.ppermute(high, "space", up)
    from_right = lax.ppermute(low, "space", down)
    left = jnp.pad(from_left, ((0, 0), (0, 0), (voxels - 64, 0)))
    right = jnp.pad(from_right, ((0, 0), (0, 0), (0, voxels - 64)))
    zero = jnp.zeros((1,) + field.shape[1:], field.dtype)
    return jnp.concatenate([field, left, right, zero])


def slot_table(neighbour_ids, my_index):
    slots = neighbour_ids.shape[0]
    dx = jnp.array([d[0] for d in DIRECTIONS], jnp.int32)[None, :]
    local = neighbour_ids - (my_index + dx) * slots
    base = jnp.where(dx == 0, 0, jnp.where(dx < 0, slots, 2 * slots))
    table = jnp.where(neighbour_ids >= 0, base + jnp.clip(local, 0, slots - 1), 3 * slots)
    return table.reshape(-1).astype(jnp.int32)


SUM_AXES = ("space", "rep")


def sum_levels(space_size, rep_size):
    z_size = 8 if space_size % 8 == 0 else space_size
    space_i = lax.axis_index("space")
    rep_i = lax.axis_index("rep")
    x_i, z_i = space_i // z_size, space_i % z_size
    levels = []
    if rep_size > 1:
        levels.append((rep_size, rep_i, lambda p: (space_i, p)))
    if z_size > 1:
        levels.append((z_size, z_i, lambda p: (x_i * z_size + p, rep_i)))
    if space_size // z_size > 1:
        levels.append((space_size // z_size, x_i, lambda p: (p * z_size + z_i, rep_i)))
    return levels


def reduce_kernel(
    space_size, rep_size, weight_rows, scale, tbl_ref, x_ref, gp_ref, cot_ref, occ_ref, wt_ref,
    o_ref, bias_out_ref, in_grad_ref, *scratch,
):
    levels = sum_levels(space_size, rep_size)
    count = len(levels)
    buf, full, col_ref, send_sem, recv_sem, local_sem, g_ref, plane_send, plane_recv = scratch[:9]
    recvs = scratch[9:]
    rows = buf.shape[0]
    slots, channels, voxels = cot_ref.shape
    edges = edge_masks((1, voxels))
    windows = 2 * count - 1
    mesh_ids = pl.DeviceIdType.MESH

    def bricks_of(window):
        for brick in range(window, slots, windows):
            backward_brick(tbl_ref, g_ref, cot_ref, occ_ref, wt_ref, in_grad_ref, col_ref, edges, brick)

    space_i = lax.axis_index("space")
    rep_i = lax.axis_index("rep")
    sides = ((space_i + 1) % space_size, (space_i + space_size - 1) % space_size)
    g_ref[pl.ds(slots, 2 * slots + 1)] = jnp.zeros((2 * slots + 1, channels, voxels), g_ref.dtype)
    g_ref[pl.ds(0, slots)] = gp_ref[...]
    barrier = pltpu.get_barrier_semaphore()
    for n, r, device in levels:
        for d in range(1, n):
            pl.semaphore_signal(barrier, 1, device_id=device((r + d) % n), device_id_type=mesh_ids)
    for side in sides:
        pl.semaphore_signal(barrier, 1, device_id=(side, rep_i), device_id_type=mesh_ids)
    pl.semaphore_wait(barrier, sum(n - 1 for n, _, _ in levels) + 2)
    planes = []
    for way, side in enumerate(sides):
        lanes = pl.ds(voxels - 128, 128) if way == 0 else pl.ds(0, 128)
        for brick in range(slots):
            copy = pltpu.make_async_remote_copy(
                src_ref=gp_ref.at[brick, :, lanes],
                dst_ref=g_ref.at[(way + 1) * slots + brick, :, lanes],
                send_sem=plane_send.at[way, brick],
                recv_sem=plane_recv.at[way, brick],
                device_id=(side, rep_i),
                device_id_type=mesh_ids,
            )
            copy.start()
            planes.append(copy)
    first = pltpu.make_async_copy(x_ref, buf, local_sem)
    first.start()
    first.wait()
    lo = 0
    length = rows
    for i, (n, r, device) in enumerate(levels[:-1]):
        chunk = length // n
        copies = []
        for d in range(1, n):
            p = (r + d) % n
            copy = pltpu.make_async_remote_copy(
                src_ref=buf.at[pl.ds(pl.multiple_of(lo + p * chunk, 8), chunk)],
                dst_ref=recvs[i].at[d],
                send_sem=send_sem.at[i, d],
                recv_sem=recv_sem.at[i, d],
                device_id=device(p),
                device_id_type=mesh_ids,
            )
            copy.start()
            copies.append(copy)
        if i == 0:
            for copy in planes:
                copy.wait()
        bricks_of(i)
        for copy in copies:
            copy.wait()
        mine = pl.multiple_of(lo + r * chunk, 8)
        total = buf[pl.ds(mine, chunk)]
        for d in range(1, n):
            total = total + recvs[i][d]
        buf[pl.ds(mine, chunk)] = total
        lo = mine
        length = chunk
    last = count - 1
    n, r, device = levels[last]
    stage = recvs[last]
    stage[0] = buf[pl.ds(lo, length)]
    copies = []
    for d in range(1, n):
        copy = pltpu.make_async_remote_copy(
            src_ref=buf.at[pl.ds(lo, length)],
            dst_ref=stage.at[d],
            send_sem=send_sem.at[last, d],
            recv_sem=recv_sem.at[last, d],
            device_id=device((r + d) % n),
            device_id_type=mesh_ids,
        )
        copy.start()
        copies.append(copy)
    bricks_of(last)
    for copy in copies:
        copy.wait()
    total = stage[(r + n) % n]
    for m in range(1, n):
        total = total + stage[(r + n - m) % n]
    full[pl.ds(lo, length)] = total
    for i in reversed(range(last)):
        n, r, device = levels[i]
        copies = []
        for d in range(1, n):
            copy = pltpu.make_async_remote_copy(
                src_ref=full.at[pl.ds(lo, length)],
                dst_ref=full.at[pl.ds(lo, length)],
                send_sem=send_sem.at[count + i, d],
                recv_sem=recv_sem.at[count + i, d],
                device_id=device((r + d) % n),
                device_id_type=mesh_ids,
            )
            copy.start()
            copies.append(copy)
        bricks_of(2 * count - 1 - 1 - i)
        for copy in copies:
            copy.wait()
        lo = pl.multiple_of(lo - r * length, 8)
        length = n * length
    o_ref[...] = full[pl.ds(0, weight_rows)] * scale
    bias_out_ref[...] = full[pl.ds(weight_rows, 8)] * scale


def all_sum_and_backward(weight_terms, bias_terms, tbl, grad_pre, incoming, keep_float, w_t, scale):
    flat = jnp.concatenate([weight_terms.reshape(-1), bias_terms])
    space_size = lax.axis_size("space")
    rep_size = lax.axis_size("rep")
    z_size = 8 if space_size % 8 == 0 else space_size
    sizes = [n for n in (rep_size, z_size, space_size // z_size) if n > 1]
    unit = 8 * math.prod(sizes[:-1])
    whole = flat.shape[0]
    rows = -(-(-(-whole // 128)) // unit) * unit
    x = jnp.pad(flat, (0, rows * 128 - whole)).reshape(rows, 128)
    recvs = []
    length = rows
    for n in sizes[:-1]:
        length //= n
        recvs.append(pltpu.VMEM((n, length, 128), jnp.float32))
    recvs.append(pltpu.VMEM((sizes[-1], length, 128), jnp.float32))
    slots, channels, voxels = incoming.shape
    weight_rows = weight_terms.size // 128
    summed, bias_rows, in_grad = pl.pallas_call(
        functools.partial(reduce_kernel, space_size, rep_size, weight_rows, scale),
        out_shape=(
            jax.ShapeDtypeStruct((weight_rows, 128), jnp.float32),
            jax.ShapeDtypeStruct((8, 128), jnp.float32),
            jax.ShapeDtypeStruct((slots, channels, voxels), jnp.bfloat16),
        ),
        in_specs=[pl.BlockSpec(memory_space=pltpu.SMEM)] + vmem_specs(5),
        out_specs=tuple(vmem_specs(3)),
        scratch_shapes=[
            pltpu.VMEM((rows, 128), jnp.float32),
            pltpu.VMEM((rows, 128), jnp.float32),
            pltpu.VMEM((27 * channels, voxels), jnp.bfloat16),
            pltpu.SemaphoreType.DMA((2 * len(sizes), max(sizes))),
            pltpu.SemaphoreType.DMA((2 * len(sizes), max(sizes))),
            pltpu.SemaphoreType.DMA(()),
            pltpu.VMEM((3 * slots + 1, channels, voxels), jnp.bfloat16),
            pltpu.SemaphoreType.DMA((2, slots)),
            pltpu.SemaphoreType.DMA((2, slots)),
        ]
        + recvs,
        compiler_params=pltpu.CompilerParams(collective_id=0, has_side_effects=True),
        interpret=REMOTE_INTERPRET,
    )(tbl, x, grad_pre, incoming, keep_float, w_t)
    return summed.reshape(weight_terms.shape), bias_rows[0, : bias_terms.size], in_grad


def on_device(feats, cotangent, weight, bias, neighbours, occupancy):
    filled = occupancy[0]
    incoming = cotangent[0]
    slot_count, channels = (feats.shape[1], feats.shape[2])
    my_index = lax.axis_index("space")
    masked = feats[0] * filled.astype(jnp.bfloat16)[:, None, :]
    keep_float = filled.astype(jnp.float32)[:, None, :]
    tbl = slot_table(neighbours[0], my_index)
    w_all = weight.transpose(1, 0, 2).reshape(channels, 27 * channels)
    w_t = weight.transpose(2, 0, 1).reshape(channels, 27 * channels)
    result, grad_pre, dw, db = run_forward(
        tbl, masked, incoming, keep_float, w_all, bias.reshape(channels, 1)
    )
    weight_terms = dw.reshape(channels, 27, channels).transpose(1, 0, 2)
    normaliser = 1.0 / math.sqrt(
        feats.shape[0] * lax.axis_size("rep") * slot_count * lax.axis_size("space") * 512
    )
    weight_total, bias_total, in_grad = all_sum_and_backward(
        weight_terms, db.reshape(channels), tbl, grad_pre, incoming, keep_float, w_t, normaliser
    )
    return (result[None], in_grad[None], weight_total, bias_total)


def solution(mesh):
    placed = (
        P("rep", "space", None, None),
        P("rep", "space", None, None),
        P(),
        P(),
        P("rep", "space", None),
        P("rep", "space", None),
    )
    return jax.shard_map(
        on_device,
        mesh=mesh,
        in_specs=placed,
        out_specs=(P("rep", "space", None, None), P("rep", "space", None, None), P(), P()),
        check_vma=False,
    )
```

```python
import functools
import math

import jax
import jax.numpy as jnp
from jax import lax
from jax.experimental import pallas as pl
from jax.experimental.pallas import tpu as pltpu
from jax.sharding import PartitionSpec as P

INTERPRET = False
REMOTE_INTERPRET = False

DIRECTIONS = [
    (a, b, c) for a in (-1, 0, 1) for b in (-1, 0, 1) for c in (-1, 0, 1) if (a, b, c) != (0, 0, 0)
]
OFFSETS = [(a - 1, b - 1, c - 1) for a in range(3) for b in range(3) for c in range(3)]
STRIDES = (64, 8, 1)
ZERO_SLOT = 12


def offset_terms(shift):
    moving = [axis for axis in range(3) if shift[axis] != 0]
    terms = []
    for pick in range(1 << len(moving)):
        out_axes = [axis for n, axis in enumerate(moving) if (pick >> n) & 1]
        direction = tuple(shift[axis] if axis in out_axes else 0 for axis in range(3))
        flat = sum(STRIDES[axis] * (shift[axis] - (8 * shift[axis] if axis in out_axes else 0)) for axis in range(3))
        pattern = [(axis, shift[axis], axis in out_axes) for axis in moving]
        terms.append((direction, (-flat) % 512, pattern))
    return terms


def gather_columns(src_ref, tbl_ref, brick, col_ref, sign, edges):
    base = brick * 26
    for k, off in enumerate(OFFSETS):
        shift = tuple(sign * s for s in off)
        val = None
        for direction, roll, pattern in offset_terms(shift):
            if direction == (0, 0, 0):
                field = src_ref[brick]
            else:
                slot = tbl_ref[base + DIRECTIONS.index(direction)]
                field = src_ref[slot]
            if roll:
                field = pltpu.roll(field, roll, 1)
            if val is None:
                val = field
                continue
            mask = None
            for axis, step, out in pattern:
                m = edges[(axis, step)] if out else jnp.logical_not(edges[(axis, step)])
                mask = m if mask is None else jnp.logical_and(mask, m)
            val = jnp.where(mask, field, val)
        col_ref[pl.ds(k * 64, 64), :] = val


def edge_masks(shape):
    v = lax.broadcasted_iota(jnp.int32, shape, 1)
    coords = (v >> 6, (v >> 3) & 7, v & 7)
    edges = {}
    for axis in range(3):
        edges[(axis, -1)] = coords[axis] == 0
        edges[(axis, 1)] = coords[axis] == 7
    return edges


def forward_kernel(
    space_size, tbl_ref, xm_ref, cot_ref, occ_ref, w_ref, bias_ref, out_ref, gp_ref, dw_ref, db_ref,
    col_ref, x_ref, plane_send, plane_recv,
):
    slots, channels, voxels = cot_ref.shape
    edges = edge_masks((1, voxels))
    space_i = lax.axis_index("space")
    rep_i = lax.axis_index("rep")
    mesh_ids = pl.DeviceIdType.MESH
    sides = ((space_i + 1) % space_size, (space_i + space_size - 1) % space_size)
    x_ref[pl.ds(slots, 2 * slots + 1)] = jnp.zeros((2 * slots + 1, channels, voxels), x_ref.dtype)
    x_ref[pl.ds(0, slots)] = xm_ref[...]
    barrier = pltpu.get_barrier_semaphore()
    for side in sides:
        pl.semaphore_signal(barrier, 1, device_id=(side, rep_i), device_id_type=mesh_ids)
    pl.semaphore_wait(barrier, 2)
    planes = []
    for way, side in enumerate(sides):
        lanes = pl.ds(voxels - 128, 128) if way == 0 else pl.ds(0, 128)
        for brick in range(slots):
            copy = pltpu.make_async_remote_copy(
                src_ref=xm_ref.at[brick, :, lanes],
                dst_ref=x_ref.at[(way + 1) * slots + brick, :, lanes],
                send_sem=plane_send.at[way, brick],
                recv_sem=plane_recv.at[way, brick],
                device_id=(side, rep_i),
                device_id_type=mesh_ids,
            )
            copy.start()
            planes.append(copy)
    for copy in planes:
        copy.wait()
    dw_ref[...] = jnp.zeros_like(dw_ref)
    db_ref[...] = jnp.zeros_like(db_ref)

    def brick_step(brick, carry):
        gather_columns(x_ref, tbl_ref, brick, col_ref, 1, edges)
        pre = jnp.dot(w_ref[...], col_ref[...], preferred_element_type=jnp.float32) + bias_ref[...]
        sig = 1.0 / (1.0 + jnp.exp(-pre))
        keep = occ_ref[brick]
        masked = x_ref[brick].astype(jnp.float32)
        out_ref[brick] = (masked + keep * pre * sig).astype(out_ref.dtype)
        gp = (cot_ref[brick].astype(jnp.float32) * keep * sig * (1.0 + pre * (1.0 - sig))).astype(jnp.bfloat16)
        gp_ref[brick] = gp
        dw_ref[...] += lax.dot_general(
            gp, col_ref[...], (((1,), (1,)), ((), ())), preferred_element_type=jnp.float32
        )
        db_ref[...] += jnp.sum(gp.astype(jnp.float32), axis=1, keepdims=True)
        return carry

    lax.fori_loop(0, slots, brick_step, 0)


def backward_brick(tbl_ref, g_ref, cot_ref, occ_ref, wt_ref, in_grad_ref, col_ref, edges, brick):
    gather_columns(g_ref, tbl_ref, brick, col_ref, -1, edges)
    back = jnp.dot(wt_ref[...], col_ref[...], preferred_element_type=jnp.float32)
    keep = occ_ref[brick]
    in_grad_ref[brick] = (keep * (cot_ref[brick].astype(jnp.float32) + back)).astype(in_grad_ref.dtype)


def vmem_specs(n):
    return [pl.BlockSpec(memory_space=pltpu.VMEM)] * n


def run_forward(tbl, masked, cot, occ, w_all, bias):
    slots, channels, voxels = cot.shape
    return pl.pallas_call(
        functools.partial(forward_kernel, lax.axis_size("space")),
        out_shape=(
            jax.ShapeDtypeStruct((slots, channels, voxels), jnp.bfloat16),
            jax.ShapeDtypeStruct((slots, channels, voxels), jnp.bfloat16),
            jax.ShapeDtypeStruct((channels, 27 * channels), jnp.float32),
            jax.ShapeDtypeStruct((channels, 1), jnp.float32),
        ),
        in_specs=[pl.BlockSpec(memory_space=pltpu.SMEM)] + vmem_specs(5),
        out_specs=tuple(vmem_specs(4)),
        scratch_shapes=[
            pltpu.VMEM((27 * channels, voxels), jnp.bfloat16),
            pltpu.VMEM((3 * slots + 1, channels, voxels), jnp.bfloat16),
            pltpu.SemaphoreType.DMA((2, slots)),
            pltpu.SemaphoreType.DMA((2, slots)),
        ],
        compiler_params=pltpu.CompilerParams(collective_id=1, has_side_effects=True),
        interpret=REMOTE_INTERPRET,
    )(tbl, masked, cot, occ, w_all, bias)


def exchange_planes(field):
    size = lax.axis_size("space")
    up = [(i, i + 1) for i in range(size - 1)]
    down = [(i + 1, i) for i in range(size - 1)]
    voxels = field.shape[-1]
    low = field[:, :, :64]
    high = field[:, :, voxels - 64 :]
    from_left = lax.ppermute(high, "space", up)
    from_right = lax.ppermute(low, "space", down)
    left = jnp.pad(from_left, ((0, 0), (0, 0), (voxels - 64, 0)))
    right = jnp.pad(from_right, ((0, 0), (0, 0), (0, voxels - 64)))
    zero = jnp.zeros((1,) + field.shape[1:], field.dtype)
    return jnp.concatenate([field, left, right, zero])


def slot_table(neighbour_ids, my_index):
    slots = neighbour_ids.shape[0]
    dx = jnp.array([d[0] for d in DIRECTIONS], jnp.int32)[None, :]
    local = neighbour_ids - (my_index + dx) * slots
    base = jnp.where(dx == 0, 0, jnp.where(dx < 0, slots, 2 * slots))
    table = jnp.where(neighbour_ids >= 0, base + jnp.clip(local, 0, slots - 1), 3 * slots)
    return table.reshape(-1).astype(jnp.int32)


SUM_AXES = ("space", "rep")


def sum_levels(space_size, rep_size):
    z_size = 8 if space_size % 8 == 0 else space_size
    space_i = lax.axis_index("space")
    rep_i = lax.axis_index("rep")
    x_i, z_i = space_i // z_size, space_i % z_size
    levels = []
    if rep_size > 1:
        levels.append((rep_size, rep_i, lambda p: (space_i, p)))
    if z_size > 1:
        levels.append((z_size, z_i, lambda p: (x_i * z_size + p, rep_i)))
    if space_size // z_size > 1:
        levels.append((space_size // z_size, x_i, lambda p: (p * z_size + z_i, rep_i)))
    return levels


def reduce_kernel(
    space_size, rep_size, weight_rows, scale, tbl_ref, x_ref, gp_ref, cot_ref, occ_ref, wt_ref,
    o_ref, bias_out_ref, in_grad_ref, *scratch,
):
    levels = sum_levels(space_size, rep_size)
    count = len(levels)
    buf, full, col_ref, send_sem, recv_sem, local_sem, g_ref, plane_send, plane_recv = scratch[:9]
    recvs = scratch[9:]
    rows = buf.shape[0]
    slots, channels, voxels = cot_ref.shape
    edges = edge_masks((1, voxels))
    windows = 2 * count - 1
    mesh_ids = pl.DeviceIdType.MESH

    def bricks_of(window):
        for brick in range(window, slots, windows):
            backward_brick(tbl_ref, g_ref, cot_ref, occ_ref, wt_ref, in_grad_ref, col_ref, edges, brick)

    space_i = lax.axis_index("space")
    rep_i = lax.axis_index("rep")
    sides = ((space_i + 1) % space_size, (space_i + space_size - 1) % space_size)
    g_ref[pl.ds(slots, 2 * slots + 1)] = jnp.zeros((2 * slots + 1, channels, voxels), g_ref.dtype)
    g_ref[pl.ds(0, slots)] = gp_ref[...]
    barrier = pltpu.get_barrier_semaphore()
    for n, r, device in levels:
        for d in range(1, n):
            pl.semaphore_signal(barrier, 1, device_id=device((r + d) % n), device_id_type=mesh_ids)
    for side in sides:
        pl.semaphore_signal(barrier, 1, device_id=(side, rep_i), device_id_type=mesh_ids)
    pl.semaphore_wait(barrier, sum(n - 1 for n, _, _ in levels) + 2)
    planes = []
    for way, side in enumerate(sides):
        lanes = pl.ds(voxels - 128, 128) if way == 0 else pl.ds(0, 128)
        for brick in range(slots):
            copy = pltpu.make_async_remote_copy(
                src_ref=gp_ref.at[brick, :, lanes],
                dst_ref=g_ref.at[(way + 1) * slots + brick, :, lanes],
                send_sem=plane_send.at[way, brick],
                recv_sem=plane_recv.at[way, brick],
                device_id=(side, rep_i),
                device_id_type=mesh_ids,
            )
            copy.start()
            planes.append(copy)
    first = pltpu.make_async_copy(x_ref, buf, local_sem)
    first.start()
    first.wait()
    lo = 0
    length = rows
    for i, (n, r, device) in enumerate(levels[:-1]):
        chunk = length // n
        copies = []
        for d in range(1, n):
            p = (r + d) % n
            copy = pltpu.make_async_remote_copy(
                src_ref=buf.at[pl.ds(pl.multiple_of(lo + p * chunk, 8), chunk)],
                dst_ref=recvs[i].at[d],
                send_sem=send_sem.at[i, d],
                recv_sem=recv_sem.at[i, d],
                device_id=device(p),
                device_id_type=mesh_ids,
            )
            copy.start()
            copies.append(copy)
        if i == 0:
            for copy in planes:
                copy.wait()
        bricks_of(i)
        for copy in copies:
            copy.wait()
        mine = pl.multiple_of(lo + r * chunk, 8)
        total = buf[pl.ds(mine, chunk)]
        for d in range(1, n):
            total = total + recvs[i][d]
        buf[pl.ds(mine, chunk)] = total
        lo = mine
        length = chunk
    last = count - 1
    n, r, device = levels[last]
    stage = recvs[last]
    stage[0] = buf[pl.ds(lo, length)]
    copies = []
    for d in range(1, n):
        copy = pltpu.make_async_remote_copy(
            src_ref=buf.at[pl.ds(lo, length)],
            dst_ref=stage.at[d],
            send_sem=send_sem.at[last, d],
            recv_sem=recv_sem.at[last, d],
            device_id=device((r + d) % n),
            device_id_type=mesh_ids,
        )
        copy.start()
        copies.append(copy)
    bricks_of(last)
    for copy in copies:
        copy.wait()
    total = stage[(r + n) % n]
    for m in range(1, n):
        total = total + stage[(r + n - m) % n]
    full[pl.ds(lo, length)] = total
    for i in reversed(range(last)):
        n, r, device = levels[i]
        copies = []
        for d in range(1, n):
            copy = pltpu.make_async_remote_copy(
                src_ref=full.at[pl.ds(lo, length)],
                dst_ref=full.at[pl.ds(lo, length)],
                send_sem=send_sem.at[count + i, d],
                recv_sem=recv_sem.at[count + i, d],
                device_id=device((r + d) % n),
                device_id_type=mesh_ids,
            )
            copy.start()
            copies.append(copy)
        bricks_of(2 * count - 1 - 1 - i)
        for copy in copies:
            copy.wait()
        lo = pl.multiple_of(lo - r * length, 8)
        length = n * length
    half = o_ref.shape[1] // 2
    width = o_ref.shape[2]
    for k in range(o_ref.shape[0]):
        block = full[pl.ds(k * half, half)] * scale
        o_ref[k, pl.ds(0, half, stride=2), :] = block[:, :width]
        o_ref[k, pl.ds(1, half, stride=2), :] = block[:, width:]
    bias_out_ref[...] = full[pl.ds(weight_rows, 8)] * scale


def all_sum_and_backward(weight_terms, bias_terms, tbl, grad_pre, incoming, keep_float, w_t, scale):
    flat = jnp.concatenate([weight_terms.reshape(-1), bias_terms])
    space_size = lax.axis_size("space")
    rep_size = lax.axis_size("rep")
    z_size = 8 if space_size % 8 == 0 else space_size
    sizes = [n for n in (rep_size, z_size, space_size // z_size) if n > 1]
    unit = 8 * math.prod(sizes[:-1])
    whole = flat.shape[0]
    rows = -(-(-(-whole // 128)) // unit) * unit
    x = jnp.pad(flat, (0, rows * 128 - whole)).reshape(rows, 128)
    recvs = []
    length = rows
    for n in sizes[:-1]:
        length //= n
        recvs.append(pltpu.VMEM((n, length, 128), jnp.float32))
    recvs.append(pltpu.VMEM((sizes[-1], length, 128), jnp.float32))
    slots, channels, voxels = incoming.shape
    weight_rows = weight_terms.size // 128
    summed, bias_rows, in_grad = pl.pallas_call(
        functools.partial(reduce_kernel, space_size, rep_size, weight_rows, scale),
        out_shape=(
            jax.ShapeDtypeStruct(weight_terms.shape, jnp.float32),
            jax.ShapeDtypeStruct((8, 128), jnp.float32),
            jax.ShapeDtypeStruct((slots, channels, voxels), jnp.bfloat16),
        ),
        in_specs=[pl.BlockSpec(memory_space=pltpu.SMEM)] + vmem_specs(5),
        out_specs=tuple(vmem_specs(3)),
        scratch_shapes=[
            pltpu.VMEM((rows, 128), jnp.float32),
            pltpu.VMEM((rows, 128), jnp.float32),
            pltpu.VMEM((27 * channels, voxels), jnp.bfloat16),
            pltpu.SemaphoreType.DMA((2 * len(sizes), max(sizes))),
            pltpu.SemaphoreType.DMA((2 * len(sizes), max(sizes))),
            pltpu.SemaphoreType.DMA(()),
            pltpu.VMEM((3 * slots + 1, channels, voxels), jnp.bfloat16),
            pltpu.SemaphoreType.DMA((2, slots)),
            pltpu.SemaphoreType.DMA((2, slots)),
        ]
        + recvs,
        compiler_params=pltpu.CompilerParams(collective_id=0, has_side_effects=True),
        interpret=REMOTE_INTERPRET,
    )(tbl, x, grad_pre, incoming, keep_float, w_t)
    return summed, bias_rows[0, : bias_terms.size], in_grad


def on_device(feats, cotangent, weight, bias, neighbours, occupancy):
    filled = occupancy[0]
    incoming = cotangent[0]
    slot_count, channels = (feats.shape[1], feats.shape[2])
    my_index = lax.axis_index("space")
    masked = feats[0] * filled.astype(jnp.bfloat16)[:, None, :]
    keep_float = filled.astype(jnp.float32)[:, None, :]
    tbl = slot_table(neighbours[0], my_index)
    w_all = weight.transpose(1, 0, 2).reshape(channels, 27 * channels)
    w_t = weight.transpose(2, 0, 1).reshape(channels, 27 * channels)
    result, grad_pre, dw, db = run_forward(
        tbl, masked, incoming, keep_float, w_all, bias.reshape(channels, 1)
    )
    weight_terms = dw.reshape(channels, 27, channels).transpose(1, 0, 2)
    normaliser = 1.0 / math.sqrt(
        feats.shape[0] * lax.axis_size("rep") * slot_count * lax.axis_size("space") * 512
    )
    weight_total, bias_total, in_grad = all_sum_and_backward(
        weight_terms, db.reshape(channels), tbl, grad_pre, incoming, keep_float, w_t, normaliser
    )
    return (result[None], in_grad[None], weight_total, bias_total)


def solution(mesh):
    placed = (
        P("rep", "space", None, None),
        P("rep", "space", None, None),
        P(),
        P(),
        P("rep", "space", None),
        P("rep", "space", None),
    )
    return jax.shard_map(
        on_device,
        mesh=mesh,
        in_specs=placed,
        out_specs=(P("rep", "space", None, None), P("rep", "space", None, None), P(), P()),
        check_vma=False,
    )
```
